256 devices in a mesh: sec: 2 (over z_hi), lat: 4 (over x), lon: 32 (over y, z_lo, core).
Axes of the slice: x: 4, y: 4, z: 8 (z_hi: 2, z_lo: 4; z = z_hi * 4 + z_lo), core: 2. Of those that a mesh axis runs over, the one named last changes fastest.
Arguments:
- spectra: float32 [36, 36, 32, 4096], P('sec', None, 'lat', 'lon'), may hold values from 0 to 2
- currents: float32 [2, 8, 32, 4096], P(None, 'sec', 'lat', 'lon'), may hold values from -3 to 3
- land_mask: int32 [32, 4096], P('lat', 'lon'), may hold values 0 or 1
- diffusion: float32 [32, 4096], P('lat', 'lon'), may hold values from 0.08 to 0.19
- courant: float32 [36], P('sec'), may hold values from 0.15 to 0.45
- stokes_weight: float32 [36], P('sec'), may hold values from 0.02 to 0.1
- stress_weight: float32 [36], P('sec'), may hold values from 0.02 to 0.1
Outputs:
- new_spectra: float32 [36, 36, 32, 4096], P('sec', None, 'lat', 'lon')
- new_currents: float32 [2, 8, 32, 4096], P(None, 'sec', 'lat', 'lon')
The draws below stay inside these ranges and needn't reach their ends.
Inputs may be any that keep to these rules, and one draw needn't show every extreme that they name: `land_mask`: 1 marks a sea column, 0 a land column.
All inputs are finite; a program needn't handle non-finite values. No bound on the sum of `land_mask` on one device may be relied on, other than what follows from the above.
Results may differ from the reference program's by a relative error of at most 0.0001.
Values sent between devices are 32-bit elements; how exact they have to be, the bound alone decides.
A program may use at most 128 MiB of HBM per device.

```python
import math
import jax
import jax.numpy as jnp
from jax import lax

FREQS = 36
DIRS = 36
ITERS = 4
LEVELS = 8
NLAT = 32
NLON = 4096


def touch_ends(values, rng, low, largest):
    index_at = [jax.random.randint(jax.random.fold_in(rng, axis), (), 0, length) for axis, length in enumerate(values.shape)]
    longest = values.shape.index(max(values.shape))
    beside = index_at[:longest] + [(index_at[longest] + 1) % values.shape[longest]] + index_at[longest + 1:]
    return values.at[tuple(index_at)].set(low).at[tuple(beside)].set(largest)


def steps_of(own_key, shape, cuts, smallest, top_value):
    loudness, own = 1.0, jax.random.fold_in(own_key, 6)
    for position, parts in cuts:
        steps = jnp.exp(jax.random.uniform(jax.random.fold_in(own, position), (parts,), jnp.float32, smallest / len(cuts), top_value / len(cuts)))
        loudness = loudness * jnp.repeat(steps, shape[position] // parts).reshape([-1 if axis == position else 1 for axis in range(len(shape))])
    return loudness


def noise(key, dims, deviation, bound, pieces=(), dtype=jnp.bfloat16):
    result = jax.random.normal(key, dims, jnp.float32) * deviation
    if len(pieces) > 0:
        result = steps_of(key, dims, pieces, -0.22, 0.18) * result
    return jnp.clip(result, min=-bound, max=bound).astype(dtype)


def setup_inputs(seed: int = 0) -> dict:
    key_list = jax.random.split(jax.random.key(seed), 8)
    spectra = jnp.clip(2.0 * jax.random.uniform(key_list[0], (FREQS, DIRS, NLAT, NLON), jnp.float32) ** steps_of(key_list[0], (FREQS, DIRS, NLAT, NLON), ((0, 2), (2, 4), (3, 32)), -0.2, 0.2), 0.0, 2.0)
    currents = noise(key_list[1], (2, LEVELS, NLAT, NLON), 1.0, 3.0, ((1, 2), (2, 4), (3, 32)), jnp.float32)
    land_mask = touch_ends((jax.random.randint(key_list[2], (NLAT, NLON), 0, 4) < 3).astype(jnp.int32), jax.random.fold_in(key_list[2], 1), 0, 1)
    diffusion = jnp.clip(0.08 + 0.11 * jax.random.uniform(key_list[3], (NLAT, NLON), jnp.float32) ** steps_of(key_list[3], (NLAT, NLON), ((0, 4), (1, 32)), -0.2, 0.2), 0.08, 0.19)
    courant = jnp.clip(0.15 + 0.29999998 * jax.random.uniform(key_list[4], (FREQS,), jnp.float32) ** steps_of(key_list[4], (FREQS,), ((0, 2),), -0.2, 0.2), 0.15, 0.45)
    stokes_weight = jnp.clip(jnp.exp(math.log(0.1) - 1.609438 * jax.random.uniform(key_list[5], (FREQS,), jnp.float32) ** steps_of(key_list[5], (FREQS,), ((0, 2),), -0.2, 0.2)), 0.02, 0.1)
    stress_weight = jnp.clip(jnp.exp(math.log(0.1) - 1.609438 * jax.random.uniform(key_list[6], (FREQS,), jnp.float32) ** steps_of(key_list[6], (FREQS,), ((0, 2),), -0.2, 0.2)), 0.02, 0.1)
    return dict(spectra=spectra, currents=currents, land_mask=land_mask, diffusion=diffusion, courant=courant, stokes_weight=stokes_weight, stress_weight=stress_weight)


current_gain = 0.1
stress_gain = 0.5


def heading_tables(directions):
    heading = (jnp.arange(directions).astype(jnp.float32) + 0.5) * (2.0 * math.pi / directions)
    return jnp.cos(heading), jnp.sin(heading)


def wave_update(energy, west_cell, east_cell, south_cell, north_cell, speed, cosine_table, sine_table, surface, sea_cells):
    speed_x = (speed[:, None] * cosine_table[None])[:, :, None, None]
    speed_y = (speed[:, None] * sine_table[None])[:, :, None, None]
    step_x = jnp.maximum(speed_x, 0.0) * (energy - west_cell) + jnp.minimum(speed_x, 0.0) * (east_cell - energy)
    step_y = jnp.maximum(speed_y, 0.0) * (energy - south_cell) + jnp.minimum(speed_y, 0.0) * (north_cell - energy)
    advected = energy - step_x - step_y
    doppler = 1.0 + current_gain * (surface[0][None] * cosine_table[:, None, None] + surface[1][None] * sine_table[:, None, None])
    return sea_cells * (advected * doppler)


def coupling_weights(stokes_w, stress_w, cosine_table, sine_table):
    stacked = jnp.stack([stokes_w[:, None] * cosine_table[None], stokes_w[:, None] * sine_table[None],
                         stress_w[:, None] * cosine_table[None], stress_w[:, None] * sine_table[None]])
    return stacked.reshape(4, stokes_w.shape[0] * cosine_table.shape[0])


def vertical_rate(level):
    return 0.04 + 0.0125 * ((7 * level) % 5).astype(jnp.float32)


def coriolis_rate(row_index, total_rows):
    return 0.05 + 0.1 * (row_index.astype(jnp.float32) + 0.5) / total_rows


def ocean_step(extended, column_data, first_level, first_row, total_levels, total_rows):
    center = extended[:, 1:-1, 1:-1, 1:-1]
    laplace = (extended[:, 1:-1, 2:, 1:-1] + extended[:, 1:-1, :-2, 1:-1]
               + extended[:, 1:-1, 1:-1, 2:] + extended[:, 1:-1, 1:-1, :-2] - 4.0 * center)
    level_above = extended[:, :-2, 1:-1, 1:-1]
    level_below = extended[:, 2:, 1:-1, 1:-1]
    level = first_level + 1 + jnp.arange(center.shape[1])
    has_up = (level > 0)[:, None, None]
    has_down = (level < total_levels - 1)[:, None, None]
    mixing = vertical_rate(level)[:, None, None]
    vertical = mixing * (jnp.where(has_up, level_above - center, 0.0) + jnp.where(has_down, level_below - center, 0.0))
    stokes_decay = (1.0 / (1.0 + level.astype(jnp.float32)))[:, None, None]
    top_gain = jnp.where(level == 0, stress_gain, 0.0)[:, None, None]
    row_index = first_row + 1 + jnp.arange(center.shape[2])
    coriolis = coriolis_rate(row_index, total_rows)[:, None]
    sea_cells = column_data[0]
    kappa = column_data[1]
    zonal = center[0]
    meridional = center[1]
    zonal_new = sea_cells * (zonal + kappa * laplace[0] + vertical[0]
                             + coriolis * (meridional + stokes_decay * column_data[3]) + top_gain * column_data[4])
    meridional_new = sea_cells * (meridional + kappa * laplace[1] + vertical[1]
                                  - coriolis * (zonal + stokes_decay * column_data[2]) + top_gain * column_data[5])
    return jnp.stack([zonal_new, meridional_new])


def reference(spectra, currents, land_mask, diffusion, courant, stokes_weight, stress_weight):
    sea_cells = land_mask.astype(jnp.float32)
    cosine_table, sine_table = heading_tables(DIRS)
    surface = currents[:, 0]

    def per_freq(summed, inputs):
        energy, speed, stokes_w, stress_w = inputs
        energy = energy[None]
        west_cell = jnp.roll(energy, 1, axis=3)
        east_cell = jnp.roll(energy, -1, axis=3)
        zero_row = jnp.zeros_like(energy[:, :, :1])
        south_cell = jnp.concatenate([zero_row, energy[:, :, :-1]], axis=2)
        north_cell = jnp.concatenate([energy[:, :, 1:], zero_row], axis=2)
        updated = wave_update(energy, west_cell, east_cell, south_cell, north_cell, speed[None],
                              cosine_table, sine_table, surface, sea_cells)
        weights = coupling_weights(stokes_w[None], stress_w[None], cosine_table, sine_table)
        summed = summed + jnp.dot(weights, updated.reshape(DIRS, NLAT * NLON),
                                  precision=lax.Precision.HIGHEST, preferred_element_type=jnp.float32)
        return summed, updated[0]

    start = jnp.zeros((4, NLAT * NLON), jnp.float32)
    summed, new_spectra = lax.scan(per_freq, start, (spectra, courant, stokes_weight, stress_weight))
    coupling = summed.reshape(4, NLAT, NLON)
    column_data = jnp.concatenate([sea_cells[None], diffusion[None], coupling], axis=0)
    fields = currents * sea_cells
    for iteration in range(ITERS):
        padded = jnp.pad(fields, ((0, 0), (1, 1), (1, 1), (0, 0)))
        padded = jnp.concatenate([padded[..., -1:], padded, padded[..., :1]], axis=3)
        fields = ocean_step(padded, column_data, -1, -1, LEVELS, NLAT)
    return new_spectra, fields
```

```python
import functools
import math

import jax
import jax.numpy as jnp
import numpy as np
from jax import lax
from jax.experimental import pallas as pl
from jax.experimental.pallas import tpu as pltpu
from jax.sharding import PartitionSpec as P

ITERS = 4
CURRENT_GAIN = 0.1
STRESS_GAIN = 0.5
MESH = pl.DeviceIdType.MESH
f32 = jnp.float32
CHUNKS = 3


def headings(directions):
    heading = ((np.arange(directions).astype(np.float32) + np.float32(0.5))
               * np.float32(2.0 * math.pi / directions)).astype(np.float64)
    return [float(np.float32(c)) for c in np.cos(heading)], [float(np.float32(s)) for s in np.sin(heading)]


def roll(x, shift, axis):
    shift = shift % x.shape[axis]
    return x if shift == 0 else pltpu.roll(x, shift, axis)


def kernel(
    freqs, dirs, levels, lats, lons,
    spec_hbm, cur_hbm, mask_hbm, diff_hbm, courant, stokes, stress,
    out_spec, out_cur,
    spec, outv, curv, maskv, diffv,
    send_rows, recv_rows, send_cols, recv_cols,
    fld, oth, rowpk, rowpk_in, colpk, colpk_in,
    cpl, cplo, rowc, rowc_in, colc, colc_in,
    dop, ext, ext2, aux, frc, outc,
    local_sem, send_sem, recv_sem,
):
    sec, lat, lon = lax.axis_index("sec"), lax.axis_index("lat"), lax.axis_index("lon")
    north_ok, south_ok = lat < lats - 1, lat > 0
    cosines, sines = headings(dirs)
    east_dirs = [d for d in range(dirs) if cosines[d] > 0]
    west_dirs = [d for d in range(dirs) if cosines[d] <= 0]
    north_dirs = [d for d in range(dirs) if sines[d] > 0]
    south_dirs = [d for d in range(dirs) if sines[d] <= 0]
    half = dirs // 2
    per_chunk = freqs // CHUNKS
    per_group = 128 // half
    groups = -(-freqs // per_group)

    def target(dsec, dlat, dlon):
        return (
            lax.rem(sec + dsec, 2),
            lat + dlat,
            lax.rem(lon + dlon + lons, lons),
        )

    def when_to(dlat, fn):
        if dlat == 0:
            fn()
        else:
            pl.when(north_ok if dlat > 0 else south_ok)(fn)

    partners = [
        (ds, dy, dx) for ds in (0, 1) for dy in (-1, 0, 1) for dx in (-1, 0, 1)
        if (ds, dy, dx) != (0, 0, 0)
    ]
    loads = [
        pltpu.make_async_copy(cur_hbm, curv, local_sem.at[0]),
        pltpu.make_async_copy(mask_hbm, maskv, local_sem.at[1]),
        pltpu.make_async_copy(diff_hbm, diffv, local_sem.at[2]),
        pltpu.make_async_copy(spec_hbm, spec, local_sem.at[3]),
    ]
    for copy in loads:
        copy.start()
    barrier = pltpu.get_barrier_semaphore()
    for ds, dy, dx in partners:
        def greet(ds=ds, dy=dy, dx=dx):
            pl.semaphore_signal(barrier, inc=1, device_id=target(ds, dy, dx), device_id_type=MESH)
        when_to(dy, greet)

    lane = lax.broadcasted_iota(jnp.int32, (8, 128), 1)
    sub = lax.broadcasted_iota(jnp.int32, (8, 128), 0)

    for copy in loads[:3]:
        copy.wait()
    sea = maskv[...].astype(f32)
    for q in range(2):
        for k in range(levels):
            fld[q * levels + k] = curv[q, k] * sea
    fld[2 * levels] = sea
    fld[2 * levels + 1] = diffv[...]
    n_fld = 2 * levels + 2

    def pack_rows(tiles, ref):
        for p in range(len(tiles) // 2):
            a, b = tiles[2 * p], tiles[2 * p + 1]
            ref[0, p] = jnp.where(sub >= 4, b, roll(a, 4, 0))
            ref[1, p] = jnp.where(sub < 4, a, roll(b, 4, 0))

    def pack_cols(tiles, ref):
        to_east = jnp.zeros((8, 128), f32)
        to_west = jnp.zeros((8, 128), f32)
        for i, tile in enumerate(tiles):
            here = (lane >= 4 * i) & (lane < 4 * i + 4)
            to_east = jnp.where(here, roll(tile, 4 * i + 4, 1), to_east)
            to_west = jnp.where(here, roll(tile, 4 * i, 1), to_west)
        ref[0] = to_east
        ref[1] = to_west

    tiles = [fld[i] for i in range(n_fld)]
    pack_rows(tiles, rowpk)
    pack_cols(tiles, colpk)

    loads[3].wait()

    def pack_freq(f, chunk, fi):
        base = f * (dirs * 8)
        for side, first, row in ((0, north_dirs[0], 7), (1, south_dirs[0], 0)):
            for start, count in ((0, 8), (8, 8), (half - 8, 8)):
                at = base + (first + start) * 8 + row
                send_rows[side, chunk, fi * half + start:fi * half + start + count, :] = spec[
                    pl.ds(at, count, stride=8), :
                ]

    for f in range(freqs):
        pack_freq(f, f // per_chunk, f % per_chunk)

    def pack_group(g, _):
        def one(m, accs):
            f = jnp.minimum(g * per_group + m, freqs - 1)
            base = f * (dirs * 8)
            out = []
            for side, chosen, extra in ((0, east_dirs, 1), (1, west_dirs, 0)):
                acc = jnp.zeros((8, 128), f32)
                for j, d in enumerate(chosen):
                    tile = spec[pl.ds(pl.multiple_of(base + d * 8, 8), 8), :]
                    acc = jnp.where(lane == j, roll(tile, j + extra, 1), acc)
                acc = pltpu.roll(acc, half * m, 1)
                here = (lane >= half * m) & (lane < half * m + half)
                out.append(jnp.where(here, acc, accs[side]))
            return tuple(out)

        zero = jnp.zeros((8, 128), f32)
        a, b = lax.fori_loop(0, per_group, one, (zero, zero))
        send_cols[0, g] = a
        send_cols[1, g] = b
        return 0

    lax.fori_loop(0, groups, pack_group, 0)

    edge = jnp.where(north_ok, 0, 6) + jnp.where(south_ok, 0, 6)
    pl.semaphore_wait(barrier, 17 - edge)

    messages = []

    def message(src, dst, ds, dy, dx):
        messages.append((src, dst, ds, dy, dx))
        return len(messages) - 1

    def make(i):
        src, dst, ds, dy, dx = messages[i]
        return pltpu.make_async_remote_copy(
            src_ref=src, dst_ref=dst, send_sem=send_sem.at[i], recv_sem=recv_sem.at[i],
            device_id=target(ds, dy, dx), device_id_type=MESH,
        )

    def start(i):
        when_to(messages[i][3], lambda: make(i).start())

    def wait_recv(i):
        when_to(-messages[i][3], lambda: make(i).wait_recv())

    def wait_send(i):
        when_to(messages[i][3], lambda: make(i).wait_send())

    center = message(fld.at[0:2 * levels], oth, 1, 0, 0)
    cols = [message(send_cols.at[s], recv_cols.at[s], 0, 0, 1 - 2 * s) for s in range(2)]
    rows = [
        [message(send_rows.at[s, c], recv_rows.at[s, c], 0, 1 - 2 * s, 0) for s in range(2)]
        for c in range(CHUNKS)
    ]

    def edge_messages(row_src, row_dst, col_src, col_dst):
        out = []
        for ds in (1, 0):
            for dy in (0, -1, 1):
                for s in range(2):
                    out.append(message(col_src.at[s], col_dst.at[ds, 1 + dy, s], ds, dy, 1 - 2 * s))
            for s in range(2):
                out.append(message(row_src.at[s], row_dst.at[ds, s], ds, 1 - 2 * s, 0))
        return out

    field_edges = edge_messages(rowpk, rowpk_in, colpk, colpk_in)
    for i in [center] + cols + rows[0]:
        start(i)
    for c in range(1, CHUNKS):
        for i in rows[c]:
            start(i)
    for i in field_edges:
        start(i)

    @pl.when(jnp.logical_not(south_ok))
    def _():
        recv_rows[0] = jnp.zeros(recv_rows.shape[1:], f32)

    @pl.when(jnp.logical_not(north_ok))
    def _():
        recv_rows[1] = jnp.zeros(recv_rows.shape[1:], f32)

    wait_recv(center)
    first = sec == 0
    su = jnp.where(first, fld[0], oth[0])
    sv = jnp.where(first, fld[levels], oth[levels])
    for d in range(dirs):
        dop[d] = sea * (1.0 + CURRENT_GAIN * (su * cosines[d] + sv * sines[d]))
    for i in cols:
        wait_recv(i)

    def wave(chunk, fi, sums):
        f = chunk * per_chunk + fi
        base = f * (dirs * 8)
        speed = jnp.full((8, 128), courant[f], f32)
        g = f // per_group
        m = f - g * per_group
        back = lax.rem(128 - half * m, 128)
        from_west = pltpu.roll(recv_cols[0, g], back, 1)
        from_east = pltpu.roll(recv_cols[1, g], back, 1)
        x_sum = jnp.zeros((8, 128), f32)
        y_sum = jnp.zeros((8, 128), f32)
        for d in range(dirs):
            at = pl.ds(pl.multiple_of(base + d * 8, 8), 8)
            tile = spec[at, :]
            if cosines[d] > 0:
                j = east_dirs.index(d)
                beside = jnp.where(lane == 0, roll(from_west, -j, 1), roll(tile, 1, 1))
            else:
                j = west_dirs.index(d)
                beside = jnp.where(lane == 127, roll(from_east, 127 - j, 1), roll(tile, -1, 1))
            if sines[d] > 0:
                row = recv_rows[0, chunk, pl.ds(fi * half + north_dirs.index(d), 1), :]
                along = jnp.where(sub == 0, row, roll(tile, 1, 0))
            else:
                row = recv_rows[1, chunk, pl.ds(fi * half + south_dirs.index(d), 1), :]
                along = jnp.where(sub == 7, row, roll(tile, -1, 0))
            step = abs(cosines[d]) * (beside - tile) + abs(sines[d]) * (along - tile)
            new = (tile + speed * step) * dop[d]
            outv[at, :] = new
            x_sum = x_sum + cosines[d] * new
            y_sum = y_sum + sines[d] * new
        a, b = stokes[f], stress[f]
        return (sums[0] + a * x_sum, sums[1] + a * y_sum, sums[2] + b * x_sum, sums[3] + b * y_sum)

    sums = (jnp.zeros((8, 128), f32),) * 4
    for c in range(CHUNKS):
        for i in rows[c]:
            wait_recv(i)
        sums = lax.fori_loop(0, per_chunk, functools.partial(wave, c), sums)
    store = pltpu.make_async_copy(outv, out_spec, local_sem.at[4])
    store.start()

    for i in range(4):
        cpl[i] = sums[i]
    pack_rows(list(sums), rowc)
    pack_cols(list(sums), colc)
    middle = message(cpl, cplo, 1, 0, 0)
    coupling_edges = [middle] + edge_messages(rowc, rowc_in, colc, colc_in)
    for i in coupling_edges:
        start(i)

    inside = jnp.where(sub < 4, north_ok.astype(jnp.int32), south_ok.astype(jnp.int32)) != 0
    zero = jnp.zeros((8, 128), f32)

    def ghost_rows(from_south, from_north, i):
        p = i // 2
        if i % 2 == 0:
            low, high = roll(from_south[p], 4, 0), from_north[p]
        else:
            low, high = from_south[p], roll(from_north[p], 4, 0)
        return jnp.where(inside, jnp.where(sub < 4, high, low), zero)

    def ghost_lanes(from_west, from_east, i):
        return jnp.where(
            lane < 4,
            roll(from_east, -4 * i, 1),
            jnp.where(lane >= 124, roll(from_west, 124 - 4 * i, 1), zero),
        )

    for i in field_edges:
        wait_recv(i)

    def packs(rows_in, cols_in, r, count):
        from_south = [rows_in[r, 0, p] for p in range(count // 2)]
        from_north = [rows_in[r, 1, p] for p in range(count // 2)]
        side = [cols_in[r, 1, s] for s in range(2)]
        corner = [
            jnp.where(inside, jnp.where(sub < 4, cols_in[r, 0, s], cols_in[r, 2, s]), zero)
            for s in range(2)
        ]
        return from_south, from_north, side, corner

    def place(ref, index, own, got, i):
        from_south, from_north, side, corner = got
        ref[index + (slice(0, 8), slice(0, 128))] = own
        ref[index + (slice(0, 8), slice(128, 256))] = ghost_lanes(side[0], side[1], i)
        ref[index + (slice(8, 16), slice(0, 128))] = ghost_rows(from_south, from_north, i)
        ref[index + (slice(8, 16), slice(128, 256))] = ghost_lanes(corner[0], corner[1], i)

    for r in range(2):
        got = packs(rowpk_in, colpk_in, r, n_fld)
        base = lax.rem(sec + r, 2) * levels
        for q in range(2):
            for k in range(levels):
                i = q * levels + k
                own = fld[i] if r == 0 else oth[i]
                place(ext, (q, base + k), own, got, i)
        if r == 0:
            place(aux, (0,), fld[2 * levels], got, 2 * levels)
            place(aux, (1,), fld[2 * levels + 1], got, 2 * levels + 1)

    total = 2 * levels
    big_sub = lax.broadcasted_iota(jnp.int32, (16, 256), 0)
    row_index = jnp.where(big_sub < 12, big_sub, big_sub - 16) + lat * 8
    aux[2] = 0.05 + 0.1 * (row_index.astype(f32) + 0.5) / (8 * lats)

    def ocean(src, dst, forced):
        def at_level(k, _):
            level = k.astype(f32)
            mix = 0.04 + 0.0125 * lax.rem(7 * k, 5).astype(f32)
            up, down = jnp.maximum(k - 1, 0), jnp.minimum(k + 1, total - 1)
            sea_x, kappa, rot = aux[0], aux[1], aux[2]
            new = []
            center = [src[0, k], src[1, k]]
            for q in range(2):
                mid = center[q]
                lap = (
                    roll(mid, -1, 0) + roll(mid, 1, 0) + roll(mid, -1, 1) + roll(mid, 1, 1)
                    - 4.0 * mid
                )
                vert = mix * ((src[q, up] - mid) + (src[q, down] - mid))
                new.append(mid + kappa * lap + vert)
            new[0] = new[0] + rot * center[1]
            new[1] = new[1] - rot * center[0]
            if forced:
                decay = jnp.full((16, 256), 1.0, f32) / (1.0 + level)
                top = jnp.where(k == 0, STRESS_GAIN, 0.0)
                new[0] = new[0] + decay * frc[1] + top * frc[2]
                new[1] = new[1] - decay * frc[0] + top * frc[3]
            dst[0, k] = sea_x * new[0]
            dst[1, k] = sea_x * new[1]
            return 0

        lax.fori_loop(0, total, at_level, 0)

    ocean(ext, ext2, False)

    for i in coupling_edges:
        wait_recv(i)
    got = [packs(rowc_in, colc_in, r, 4) for r in range(2)]
    both = jax.tree.map(lambda a, b: a + b, got[0], got[1])
    for i in range(4):
        place(frc, (i,), cpl[i] + cplo[i], both, i)
    frc[0] = frc[0] * aux[2]
    frc[1] = frc[1] * aux[2]

    def add_forcing(k, _):
        decay = jnp.full((16, 256), 1.0, f32) / (1.0 + k.astype(f32))
        top = jnp.where(k == 0, STRESS_GAIN, 0.0)
        ext2[0, k] = ext2[0, k] + aux[0] * (decay * frc[1] + top * frc[2])
        ext2[1, k] = ext2[1, k] + aux[0] * (top * frc[3] - decay * frc[0])
        return 0

    lax.fori_loop(0, total, add_forcing, 0)
    src, dst = ext2, ext
    for _ in range(ITERS - 1):
        ocean(src, dst, True)
        src, dst = dst, src
    for q in range(2):
        for k in range(levels):
            outc[q, k] = src[q, sec * levels + k, 0:8, 0:128]
    store_cur = pltpu.make_async_copy(outc, out_cur, local_sem.at[0])
    store_cur.start()
    for i in range(len(messages)):
        wait_send(i)
    store_cur.wait()
    store.wait()


def shards(lats, lons, spectra, currents, land_mask, diffusion, courant, stokes_weight, stress_weight):
    freqs, dirs, tile_rows, tile_cols = spectra.shape
    levels = currents.shape[1]
    cells = freqs * dirs * tile_rows
    half = dirs // 2
    rows = -(-freqs // CHUNKS * half // 8) * 8
    groups = -(-freqs // (128 // half))
    n_fld = 2 * levels + 2
    tile = (8, 128)
    vmem = lambda *shape: pltpu.VMEM(shape, f32)
    any_spec = pl.BlockSpec(memory_space=pl.ANY)
    smem_spec = pl.BlockSpec(memory_space=pltpu.SMEM)
    n_msg = 3 + 2 * CHUNKS + 16 + 17
    new_spectra, new_currents = pl.pallas_call(
        functools.partial(kernel, freqs, dirs, levels, lats, lons),
        out_shape=(
            jax.ShapeDtypeStruct((cells, tile_cols), f32),
            jax.ShapeDtypeStruct(currents.shape, f32),
        ),
        in_specs=[any_spec] * 4 + [smem_spec] * 3,
        out_specs=(any_spec, any_spec),
        scratch_shapes=[
            vmem(cells, 128), vmem(cells, 128), vmem(2, levels, *tile),
            pltpu.VMEM(tile, jnp.int32), vmem(*tile),
            vmem(2, CHUNKS, rows, 128), vmem(2, CHUNKS, rows, 128),
            vmem(2, groups, *tile), vmem(2, groups, *tile),
            vmem(n_fld, *tile), vmem(2 * levels, *tile),
            vmem(2, n_fld // 2, *tile), vmem(2, 2, n_fld // 2, *tile),
            vmem(2, *tile), vmem(2, 3, 2, *tile),
            vmem(4, *tile), vmem(4, *tile),
            vmem(2, 2, *tile), vmem(2, 2, 2, *tile),
            vmem(2, *tile), vmem(2, 3, 2, *tile),
            vmem(dirs, *tile),
            vmem(2, 2 * levels, 16, 256), vmem(2, 2 * levels, 16, 256),
            vmem(3, 16, 256), vmem(4, 16, 256), vmem(2, levels, *tile),
            pltpu.SemaphoreType.DMA((5,)),
            pltpu.SemaphoreType.DMA((n_msg,)),
            pltpu.SemaphoreType.DMA((n_msg,)),
        ],
        compiler_params=pltpu.CompilerParams(collective_id=0, has_side_effects=True),
        name="window",
    )(spectra.reshape(cells, tile_cols), currents, land_mask, diffusion, courant, stokes_weight, stress_weight)
    return new_spectra.reshape(spectra.shape), new_currents


def solution(mesh):
    in_specs = (
        P("sec", None, "lat", "lon"),
        P(None, "sec", "lat", "lon"),
        P("lat", "lon"),
        P("lat", "lon"),
        P("sec"),
        P("sec"),
        P("sec"),
    )
    out_specs = (P("sec", None, "lat", "lon"), P(None, "sec", "lat", "lon"))
    body = functools.partial(shards, mesh.shape["lat"], mesh.shape["lon"])
    return jax.shard_map(body, mesh=mesh, in_specs=in_specs, out_specs=out_specs, check_vma=False)
```

```python
import functools
import math

import jax
import jax.numpy as jnp
import numpy as np
from jax import lax
from jax.experimental import pallas as pl
from jax.experimental.pallas import tpu as pltpu
from jax.sharding import PartitionSpec as P

ITERS = 4
CURRENT_GAIN = 0.1
STRESS_GAIN = 0.5
MESH = pl.DeviceIdType.MESH
f32 = jnp.float32
CHUNKS = 3
EMIT = 4


def headings(directions):
    heading = ((np.arange(directions).astype(np.float32) + np.float32(0.5))
               * np.float32(2.0 * math.pi / directions)).astype(np.float64)
    return [float(np.float32(c)) for c in np.cos(heading)], [float(np.float32(s)) for s in np.sin(heading)]


def roll(x, shift, axis):
    shift = shift % x.shape[axis]
    return x if shift == 0 else pltpu.roll(x, shift, axis)


def kernel(
    freqs, dirs, levels, lats, lons,
    spec_hbm, cur_hbm, mask_hbm, diff_hbm, courant_hbm, stokes_hbm, stress_hbm,
    out_spec, ext2, aux, frc,
    spec, curv, maskv, diffv, courant, stokes, stress, table,
    send_rows, recv_rows, send_cols, recv_cols,
    fld, oth, rowpk, rowpk_in, colpk, colpk_in,
    cpl, cplo, rowc, rowc_in, colc, colc_in,
    dop, acc, ext, pats, rims,
    local_sem, send_sem, recv_sem,
):
    sec, lat, lon = lax.axis_index("sec"), lax.axis_index("lat"), lax.axis_index("lon")
    north_ok, south_ok = lat < lats - 1, lat > 0
    cosines, sines = headings(dirs)
    east_dirs = [d for d in range(dirs) if cosines[d] > 0]
    west_dirs = [d for d in range(dirs) if cosines[d] <= 0]
    north_dirs = [d for d in range(dirs) if sines[d] > 0]
    south_dirs = [d for d in range(dirs) if sines[d] <= 0]
    half = dirs // 2
    per_chunk = freqs // CHUNKS
    per_group = 128 // half
    groups = -(-freqs // per_group)

    def target(dsec, dlat, dlon):
        return (
            lax.rem(sec + dsec, 2),
            lat + dlat,
            lax.rem(lon + dlon + lons, lons),
        )

    def when_to(dlat, fn):
        if dlat == 0:
            fn()
        else:
            pl.when(north_ok if dlat > 0 else south_ok)(fn)

    partners = [
        (ds, dy, dx) for ds in (0, 1) for dy in (-1, 0, 1) for dx in (-1, 0, 1)
        if (ds, dy, dx) != (0, 0, 0)
    ]
    loads = [
        pltpu.make_async_copy(cur_hbm, curv, local_sem.at[0]),
        pltpu.make_async_copy(mask_hbm, maskv, local_sem.at[1]),
        pltpu.make_async_copy(diff_hbm, diffv, local_sem.at[2]),
        pltpu.make_async_copy(spec_hbm, spec, local_sem.at[3]),
        pltpu.make_async_copy(courant_hbm, courant, local_sem.at[4]),
        pltpu.make_async_copy(stokes_hbm, stokes, local_sem.at[5]),
        pltpu.make_async_copy(stress_hbm, stress, local_sem.at[6]),
    ]
    for copy in loads:
        copy.start()
    barrier = pltpu.get_barrier_semaphore()
    for ds, dy, dx in partners:
        def greet(ds=ds, dy=dy, dx=dx):
            pl.semaphore_signal(barrier, inc=1, device_id=target(ds, dy, dx), device_id_type=MESH)
        when_to(dy, greet)

    lane = lax.broadcasted_iota(jnp.int32, (8, 128), 1)
    sub = lax.broadcasted_iota(jnp.int32, (8, 128), 0)

    for copy in loads[:3]:
        copy.wait()
    sea = maskv[...].astype(f32)
    for q in range(2):
        for k in range(levels):
            fld[q * levels + k] = curv[q, k] * sea
    fld[2 * levels] = sea
    fld[2 * levels + 1] = diffv[...]
    n_fld = 2 * levels + 2

    def pack_rows(tiles, ref):
        for p in range(len(tiles) // 2):
            a, b = tiles[2 * p], tiles[2 * p + 1]
            ref[0, p] = jnp.where(sub >= 4, b, roll(a, 4, 0))
            ref[1, p] = jnp.where(sub < 4, a, roll(b, 4, 0))

    def pack_cols(tiles, ref):
        to_east = jnp.zeros((8, 128), f32)
        to_west = jnp.zeros((8, 128), f32)
        for i, tile in enumerate(tiles):
            here = (lane >= 4 * i) & (lane < 4 * i + 4)
            to_east = jnp.where(here, roll(tile, 4 * i + 4, 1), to_east)
            to_west = jnp.where(here, roll(tile, 4 * i, 1), to_west)
        ref[0] = to_east
        ref[1] = to_west

    tiles = [fld[i] for i in range(n_fld)]
    pack_rows(tiles, rowpk)
    pack_cols(tiles, colpk)

    loads[3].wait()

    def pack_freq(f, chunk, fi):
        base = f * (dirs * 8)
        for side, first, row in ((0, north_dirs[0], 7), (1, south_dirs[0], 0)):
            for start, count in ((0, 8), (8, 8), (half - 8, 8)):
                at = base + (first + start) * 8 + row
                send_rows[side, chunk, fi * half + start:fi * half + start + count, :] = spec[
                    pl.ds(at, count, stride=8), :
                ]

    for f in range(freqs):
        pack_freq(f, f // per_chunk, f % per_chunk)

    def pack_group(g, _):
        def one(m, accs):
            f = jnp.minimum(g * per_group + m, freqs - 1)
            base = f * (dirs * 8)
            out = []
            for side, chosen, extra in ((0, east_dirs, 1), (1, west_dirs, 0)):
                acc = jnp.zeros((8, 128), f32)
                for j, d in enumerate(chosen):
                    tile = spec[pl.ds(pl.multiple_of(base + d * 8, 8), 8), :]
                    acc = jnp.where(lane == j, roll(tile, j + extra, 1), acc)
                acc = pltpu.roll(acc, half * m, 1)
                here = (lane >= half * m) & (lane < half * m + half)
                out.append(jnp.where(here, acc, accs[side]))
            return tuple(out)

        zero = jnp.zeros((8, 128), f32)
        a, b = lax.fori_loop(0, per_group, one, (zero, zero))
        send_cols[0, g] = a
        send_cols[1, g] = b
        return 0

    lax.fori_loop(0, groups, pack_group, 0)

    for copy in loads[4:]:
        copy.wait()
    member = lane // half
    place_in = lane - member * half
    for g in range(groups):
        for n, ref in enumerate((courant, stokes, stress)):
            value = jnp.zeros((8, 128), f32)
            for m in range(per_group):
                if g * per_group + m < freqs:
                    value = jnp.where(member == m, ref[g * per_group + m], value)
            pats[n * groups + g] = value
    for side, chosen in enumerate((east_dirs, west_dirs)):
        for n, values in enumerate((cosines, sines)):
            value = jnp.zeros((8, 128), f32)
            for j, d in enumerate(chosen):
                value = jnp.where(place_in == j, values[d], value)
            pats[3 * groups + 2 * side + n] = value
    for d in range(dirs):
        table[0, d] = abs(cosines[d])
        table[1, d] = abs(sines[d])

    edge = jnp.where(north_ok, 0, 6) + jnp.where(south_ok, 0, 6)
    pl.semaphore_wait(barrier, 17 - edge)

    messages = []

    def message(src, dst, ds, dy, dx):
        messages.append((src, dst, ds, dy, dx))
        return len(messages) - 1

    def make(i):
        src, dst, ds, dy, dx = messages[i]
        return pltpu.make_async_remote_copy(
            src_ref=src, dst_ref=dst, send_sem=send_sem.at[i], recv_sem=recv_sem.at[i],
            device_id=target(ds, dy, dx), device_id_type=MESH,
        )

    def start(i):
        when_to(messages[i][3], lambda: make(i).start())

    def wait_recv(i):
        when_to(-messages[i][3], lambda: make(i).wait_recv())

    def wait_send(i):
        when_to(messages[i][3], lambda: make(i).wait_send())

    center = message(fld.at[0:2 * levels], oth, 1, 0, 0)
    cols = [message(send_cols.at[s], recv_cols.at[s], 0, 0, 1 - 2 * s) for s in range(2)]
    rows = [
        [message(send_rows.at[s, c], recv_rows.at[s, c], 0, 1 - 2 * s, 0) for s in range(2)]
        for c in range(CHUNKS)
    ]

    def edge_messages(row_src, row_dst, col_src, col_dst):
        out = []
        for ds in (1, 0):
            for dy in (0, -1, 1):
                for s in range(2):
                    out.append(message(col_src.at[s], col_dst.at[ds, 1 + dy, s], ds, dy, 1 - 2 * s))
            for s in range(2):
                out.append(message(row_src.at[s], row_dst.at[ds, s], ds, 1 - 2 * s, 0))
        return out

    field_edges = edge_messages(rowpk, rowpk_in, colpk, colpk_in)
    for i in [center] + cols + rows[0]:
        start(i)
    for c in range(1, CHUNKS):
        for i in rows[c]:
            start(i)
    for i in field_edges:
        start(i)

    @pl.when(jnp.logical_not(south_ok))
    def _():
        recv_rows[0] = jnp.zeros(recv_rows.shape[1:], f32)

    @pl.when(jnp.logical_not(north_ok))
    def _():
        recv_rows[1] = jnp.zeros(recv_rows.shape[1:], f32)

    quadrants = []
    for d in range(dirs):
        kind = (cosines[d] > 0, sines[d] > 0)
        if quadrants and quadrants[-1][0] == kind:
            quadrants[-1][2] += 1
        else:
            quadrants.append([kind, d, 1])

    def wave(chunk):
        f0 = chunk * per_chunk
        speeds = [jnp.full((8, 128), courant[f0 + i], f32) for i in range(per_chunk)]
        firsts = [jnp.full((8, 128), stokes[f0 + i], f32) for i in range(per_chunk)]
        seconds = [jnp.full((8, 128), stress[f0 + i], f32) for i in range(per_chunk)]
        for (to_east, to_north), d0, count in quadrants:
            group = max(g for g in range(1, 4) if count % g == 0)
            rim = 0 if to_north else 1
            row0 = (north_dirs if to_north else south_dirs)[0]

            def body(step, _):
                for n in range(group):
                    d = d0 + step * group + n
                    along_x, along_y = table[0, d], table[1, d]
                    if chunk == 0:
                        a1 = jnp.zeros((8, 128), f32)
                        a2 = jnp.zeros((8, 128), f32)
                    else:
                        a1, a2 = acc[0, d], acc[1, d]
                    for fi in range(per_chunk):
                        at = pl.ds(pl.multiple_of((f0 + fi) * dirs * 8 + d * 8, 8), 8)
                        tile = spec[at, :]
                        beside = roll(tile, 1 if to_east else -1, 1)
                        row = recv_rows[rim, chunk, pl.ds(fi * half + d - row0, 1), :]
                        if to_north:
                            along = jnp.where(sub == 0, row, roll(tile, 1, 0))
                        else:
                            along = jnp.where(sub == 7, row, roll(tile, -1, 0))
                        change = along_x * (beside - tile) + along_y * (along - tile)
                        moved = tile + speeds[fi] * change
                        out_spec[at, :] = moved
                        a1 = a1 + firsts[fi] * moved
                        a2 = a2 + seconds[fi] * moved
                    acc[0, d] = a1
                    acc[1, d] = a2
                return 0

            lax.fori_loop(0, count // group, body, 0)

    for c in range(CHUNKS):
        for i in rows[c]:
            wait_recv(i)
        wave(c)

    wait_recv(center)
    first = sec == 0
    su = jnp.where(first, fld[0], oth[0])
    sv = jnp.where(first, fld[levels], oth[levels])
    sums = [jnp.zeros((8, 128), f32)] * 4
    for d in range(dirs):
        factor = sea * (1.0 + CURRENT_GAIN * (su * cosines[d] + sv * sines[d]))
        dop[d] = factor
        a1, a2 = factor * acc[0, d], factor * acc[1, d]
        sums[0] = sums[0] + cosines[d] * a1
        sums[1] = sums[1] + sines[d] * a1
        sums[2] = sums[2] + cosines[d] * a2
        sums[3] = sums[3] + sines[d] * a2

    for i in cols:
        wait_recv(i)
    for side in range(2):
        at = 0 if side == 0 else 127
        cos_l, sin_l = pats[3 * groups + 2 * side], pats[3 * groups + 2 * side + 1]
        wide = lambda x: jnp.broadcast_to(x[:, at:at + 1], (8, 128))
        factor = wide(sea) * (1.0 + CURRENT_GAIN * (wide(su) * cos_l + wide(sv) * sin_l))
        s1 = jnp.zeros((8, 128), f32)
        s2 = jnp.zeros((8, 128), f32)
        for g in range(groups):
            rim = pats[g] * jnp.abs(cos_l) * (recv_cols[side, g] - send_cols[side, g])
            rims[side, g] = rim
            s1 = s1 + pats[groups + g] * (rim * factor)
            s2 = s2 + pats[2 * groups + g] * (rim * factor)
        for n, part in enumerate((s1 * cos_l, s1 * sin_l, s2 * cos_l, s2 * sin_l)):
            extra = jnp.broadcast_to(jnp.sum(part, axis=1, keepdims=True), (8, 128))
            sums[n] = sums[n] + jnp.where(lane == at, extra, 0.0)

    for i in range(4):
        cpl[i] = sums[i]
    pack_rows(sums, rowc)
    pack_cols(sums, colc)
    middle = message(cpl, cplo, 1, 0, 0)
    coupling_edges = [middle] + edge_messages(rowc, rowc_in, colc, colc_in)
    for i in coupling_edges:
        start(i)

    def finish(f, _):
        base = f * (dirs * 8)
        g = f // per_group
        m = f - g * per_group
        back = lax.rem(128 - half * m, 128)
        from_west = pltpu.roll(rims[0, g], back, 1)
        from_east = pltpu.roll(rims[1, g], back, 1)
        for d in range(dirs):
            at = pl.ds(pl.multiple_of(base + d * 8, 8), 8)
            if cosines[d] > 0:
                extra = jnp.where(lane == 0, roll(from_west, -east_dirs.index(d), 1), 0.0)
            else:
                extra = jnp.where(lane == 127, roll(from_east, 127 - west_dirs.index(d), 1), 0.0)
            out_spec[at, :] = (out_spec[at, :] + extra) * dop[d]
        return 0

    lax.fori_loop(0, freqs, finish, 0)

    inside = jnp.where(sub < 4, north_ok.astype(jnp.int32), south_ok.astype(jnp.int32)) != 0
    zero = jnp.zeros((8, 128), f32)

    def ghost_rows(from_south, from_north, i):
        p = i // 2
        if i % 2 == 0:
            low, high = roll(from_south[p], 4, 0), from_north[p]
        else:
            low, high = from_south[p], roll(from_north[p], 4, 0)
        return jnp.where(inside, jnp.where(sub < 4, high, low), zero)

    def ghost_lanes(from_west, from_east, i):
        return jnp.where(
            lane < 4,
            roll(from_east, -4 * i, 1),
            jnp.where(lane >= 124, roll(from_west, 124 - 4 * i, 1), zero),
        )

    for i in field_edges:
        wait_recv(i)

    def packs(rows_in, cols_in, r, count):
        from_south = [rows_in[r, 0, p] for p in range(count // 2)]
        from_north = [rows_in[r, 1, p] for p in range(count // 2)]
        side = [cols_in[r, 1, s] for s in range(2)]
        corner = [
            jnp.where(inside, jnp.where(sub < 4, cols_in[r, 0, s], cols_in[r, 2, s]), zero)
            for s in range(2)
        ]
        return from_south, from_north, side, corner

    def place(ref, index, own, got, i):
        from_south, from_north, side, corner = got
        ref[index + (slice(0, 8), slice(0, 128))] = own
        ref[index + (slice(0, 8), slice(128, 256))] = ghost_lanes(side[0], side[1], i)
        ref[index + (slice(8, 16), slice(0, 128))] = ghost_rows(from_south, from_north, i)
        ref[index + (slice(8, 16), slice(128, 256))] = ghost_lanes(corner[0], corner[1], i)

    for r in range(2):
        got = packs(rowpk_in, colpk_in, r, n_fld)
        for q in range(2):
            for k in range(levels):
                i = q * levels + k
                own = fld[i] if r == 0 else oth[i]
                position = r * levels + jnp.where(first, k, levels - 1 - k)
                place(ext, (q, position), own, got, i)
        if r == 0:
            place(aux, (0,), fld[2 * levels], got, 2 * levels)
            place(aux, (1,), fld[2 * levels + 1], got, 2 * levels + 1)

    big_sub = lax.broadcasted_iota(jnp.int32, (16, 256), 0)
    row_index = jnp.where(big_sub < 12, big_sub, big_sub - 16) + lat * 8
    aux[2] = 0.05 + 0.1 * (row_index.astype(f32) + 0.5) / (8 * lats)

    total = 2 * levels

    def at_level(p, _):
        ocean_level(ext, ext2, aux, None, first, total, p)
        return 0

    ocean_level(ext, ext2, aux, None, first, total, 0)
    lax.fori_loop(1, total - 1, at_level, 0)

    for i in coupling_edges:
        wait_recv(i)
    got = [packs(rowc_in, colc_in, r, 4) for r in range(2)]
    both = jax.tree.map(lambda a, b: a + b, got[0], got[1])
    for i in range(4):
        place(frc, (i,), cpl[i] + cplo[i], both, i)
    for i in range(len(messages)):
        wait_send(i)


def level_of(first, total, p):
    return jnp.where(first, p, total - 1 - p)


def forcing(aux, frc, first, total, p):
    k = level_of(first, total, p)
    decay = aux[2] / (1.0 + k.astype(f32))
    top = jnp.where(k == 0, STRESS_GAIN, 0.0)
    return decay * frc[1] + top * frc[2], top * frc[3] - decay * frc[0]


def ocean_level(src, dst, aux, frc, first, total, p):
    k = level_of(first, total, p)
    mix = 0.04 + 0.0125 * lax.rem(7 * k, 5).astype(f32)
    center = [src[0, p], src[1, p]]
    new = []
    for q in range(2):
        mid = center[q]
        lap = (
            roll(mid, -1, 0) + roll(mid, 1, 0) + roll(mid, -1, 1) + roll(mid, 1, 1) - 4.0 * mid
        )
        vert = src[q, p + 1] - mid
        if not (isinstance(p, int) and p == 0):
            vert = vert + (src[q, p - 1] - mid)
        new.append(mid + aux[1] * lap + mix * vert)
    new[0] = new[0] + aux[2] * center[1]
    new[1] = new[1] - aux[2] * center[0]
    if frc is not None:
        force = forcing(aux, frc, first, total, p)
        new = [new[0] + force[0], new[1] + force[1]]
    for q in range(2):
        if dst.shape[-1] == 256:
            dst[q, p] = aux[0] * new[q]
        else:
            own = jnp.where(first, p, dst.shape[1] - 1 - p)
            dst[q, own] = (aux[0] * new[q])[0:8, 0:128]


def emit(levels, spec, ext2, aux, frc, out_spec, out_cur, fa, fb, cur, sems):
    part = spec.shape[0] // EMIT
    copies = []
    for i in range(EMIT):
        at = pl.ds(i * part, part)
        copies.append(pltpu.make_async_copy(spec.at[at], out_spec.at[at], sems.at[i]))
    for copy in copies:
        copy.start()
    first = lax.axis_index("sec") == 0
    total = 2 * levels
    for p in range(total - 1):
        force = forcing(aux, frc, first, total, p)
        for q in range(2):
            fa[q, p] = ext2[q, p] + aux[0] * force[q]
    src, dst = fa, fb
    for step in range(1, ITERS):
        for p in range(total - 1 - step):
            ocean_level(src, cur if step == ITERS - 1 else dst, aux, frc, first, total, p)
        src, dst = dst, src
    last = pltpu.make_async_copy(cur, out_cur, sems.at[EMIT])
    last.start()
    for copy in copies:
        copy.wait()
    last.wait()


def shards(lats, lons, spectra, currents, land_mask, diffusion, courant, stokes_weight, stress_weight):
    freqs, dirs, tile_rows, tile_cols = spectra.shape
    levels = currents.shape[1]
    cells = freqs * dirs * tile_rows
    half = dirs // 2
    rows = -(-freqs // CHUNKS * half // 8) * 8
    groups = -(-freqs // (128 // half))
    n_fld = 2 * levels + 2
    tile = (8, 128)
    vmem = lambda *shape: pltpu.VMEM(shape, f32)
    any_spec = pl.BlockSpec(memory_space=pl.ANY)
    n_msg = 3 + 2 * CHUNKS + 16 + 17
    big = (2, 2 * levels, 16, 256)
    vmem_spec = pl.BlockSpec(memory_space=pltpu.VMEM)
    results = pl.pallas_call(
        functools.partial(kernel, freqs, dirs, levels, lats, lons),
        out_shape=(vmem(cells, 128), vmem(*big), vmem(3, 16, 256), vmem(4, 16, 256)),
        in_specs=[any_spec] * 7,
        out_specs=(vmem_spec,) * 4,
        scratch_shapes=[
            vmem(cells, 128), vmem(2, levels, *tile),
            pltpu.VMEM(tile, jnp.int32), vmem(*tile),
            pltpu.SMEM((freqs,), f32), pltpu.SMEM((freqs,), f32), pltpu.SMEM((freqs,), f32),
            pltpu.SMEM((2, dirs), f32),
            vmem(2, CHUNKS, rows, 128), vmem(2, CHUNKS, rows, 128),
            vmem(2, groups, *tile), vmem(2, groups, *tile),
            vmem(n_fld, *tile), vmem(2 * levels, *tile),
            vmem(2, n_fld // 2, *tile), vmem(2, 2, n_fld // 2, *tile),
            vmem(2, *tile), vmem(2, 3, 2, *tile),
            vmem(4, *tile), vmem(4, *tile),
            vmem(2, 2, *tile), vmem(2, 2, 2, *tile),
            vmem(2, *tile), vmem(2, 3, 2, *tile),
            vmem(dirs, *tile), vmem(2, dirs, *tile), vmem(*big),
            vmem(3 * groups + 4, *tile), vmem(2, groups, *tile),
            pltpu.SemaphoreType.DMA((7,)),
            pltpu.SemaphoreType.DMA((n_msg,)),
            pltpu.SemaphoreType.DMA((n_msg,)),
        ],
        compiler_params=pltpu.CompilerParams(collective_id=0, has_side_effects=True),
        name="window",
    )(spectra.reshape(cells, tile_cols), currents, land_mask, diffusion, courant, stokes_weight, stress_weight)
    results = [pltpu.with_memory_space_constraint(r, pltpu.VMEM) for r in results]
    new_spectra, new_currents = pl.pallas_call(
        functools.partial(emit, levels),
        out_shape=(
            jax.ShapeDtypeStruct((cells, tile_cols), f32),
            jax.ShapeDtypeStruct(currents.shape, f32),
        ),
        in_specs=[vmem_spec] * 4,
        out_specs=(any_spec, any_spec),
        scratch_shapes=[
            vmem(*big), vmem(*big), vmem(2, levels, *tile), pltpu.SemaphoreType.DMA((EMIT + 1,)),
        ],
        name="emit",
    )(*results)
    return new_spectra.reshape(spectra.shape), new_currents


def solution(mesh):
    in_specs = (
        P("sec", None, "lat", "lon"),
        P(None, "sec", "lat", "lon"),
        P("lat", "lon"),
        P("lat", "lon"),
        P("sec"),
        P("sec"),
        P("sec"),
    )
    out_specs = (P("sec", None, "lat", "lon"), P(None, "sec", "lat", "lon"))
    body = functools.partial(shards, mesh.shape["lat"], mesh.shape["lon"])
    return jax.shard_map(body, mesh=mesh, in_specs=in_specs, out_specs=out_specs, check_vma=False)
```

```python
import functools
import math

import jax
import jax.numpy as jnp
import numpy as np
from jax import lax
from jax.experimental import pallas as pl
from jax.experimental.pallas import tpu as pltpu
from jax.sharding import PartitionSpec as P

ITERS = 4
CURRENT_GAIN = 0.1
STRESS_GAIN = 0.5
MESH = pl.DeviceIdType.MESH
f32 = jnp.float32
CHUNKS = 3
EMIT = 4


def headings(directions):
    heading = ((np.arange(directions).astype(np.float32) + np.float32(0.5))
               * np.float32(2.0 * math.pi / directions)).astype(np.float64)
    return [float(np.float32(c)) for c in np.cos(heading)], [float(np.float32(s)) for s in np.sin(heading)]


def roll(x, shift, axis):
    shift = shift % x.shape[axis]
    return x if shift == 0 else pltpu.roll(x, shift, axis)


def kernel(
    freqs, dirs, levels, lats, lons,
    spec_hbm, cur_hbm, mask_hbm, diff_hbm, courant_hbm, stokes_hbm, stress_hbm,
    out_spec, ext2, aux, frc,
    spec, curv, maskv, diffv, courant, stokes, stress, table,
    send_rows, recv_rows, send_cols, recv_cols,
    own, oth, edges, rowpk, row_in, colpk, col_in,
    cpl, cplo, rowc, rowc_in, colc, colc_in,
    dop, acc, gsum, sums, hrow, hrow_in, hcol, hcol_in, ext,
    local_sem, send_sem, recv_sem, ready,
):
    sec, lat, lon = lax.axis_index("sec"), lax.axis_index("lat"), lax.axis_index("lon")
    north_ok, south_ok = lat < lats - 1, lat > 0
    cosines, sines = headings(dirs)
    east_dirs = [d for d in range(dirs) if cosines[d] > 0]
    west_dirs = [d for d in range(dirs) if cosines[d] <= 0]
    north_dirs = [d for d in range(dirs) if sines[d] > 0]
    south_dirs = [d for d in range(dirs) if sines[d] <= 0]
    half = dirs // 2
    per_chunk = freqs // CHUNKS
    per_group = 128 // half
    groups = -(-freqs // per_group)

    def target(dsec, dlat, dlon):
        return (
            lax.rem(sec + dsec, 2),
            lat + dlat,
            lax.rem(lon + dlon + lons, lons),
        )

    def when_to(dlat, fn):
        if dlat == 0:
            fn()
        else:
            pl.when(north_ok if dlat > 0 else south_ok)(fn)

    partners = [
        (ds, dy, dx) for ds in (0, 1) for dy in (-1, 0, 1) for dx in (-1, 0, 1)
        if (ds, dy, dx) == (1, 0, 0) or (ds == 0 and (dy, dx) != (0, 0))
    ]
    loads = [
        pltpu.make_async_copy(cur_hbm, curv, local_sem.at[0]),
        pltpu.make_async_copy(mask_hbm, maskv, local_sem.at[1]),
        pltpu.make_async_copy(diff_hbm, diffv, local_sem.at[2]),
        pltpu.make_async_copy(spec_hbm, spec, local_sem.at[3]),
        pltpu.make_async_copy(courant_hbm, courant, local_sem.at[4]),
        pltpu.make_async_copy(stokes_hbm, stokes, local_sem.at[5]),
        pltpu.make_async_copy(stress_hbm, stress, local_sem.at[6]),
    ]
    for copy in loads:
        copy.start()
    barrier = pltpu.get_barrier_semaphore()
    for ds, dy, dx in partners:
        def greet(ds=ds, dy=dy, dx=dx):
            pl.semaphore_signal(barrier, inc=1, device_id=target(ds, dy, dx), device_id_type=MESH)
        when_to(dy, greet)

    lane = lax.broadcasted_iota(jnp.int32, (8, 128), 1)
    sub = lax.broadcasted_iota(jnp.int32, (8, 128), 0)

    first = sec == 0
    for copy in loads[:3]:
        copy.wait()
    sea = maskv[...].astype(f32)
    for q in range(2):
        for p in range(levels):
            own[q * levels + p] = curv[q, jnp.where(first, p, levels - 1 - p)] * sea
    edges[0] = sea
    edges[1] = diffv[...]
    n_fld, n_sum = 2 * levels, 10

    loads[3].wait()

    def pack_freq(f, chunk, fi):
        base = f * (dirs * 8)
        for side, start_dir, row in ((0, north_dirs[0], 7), (1, south_dirs[0], 0)):
            for start, count in ((0, 8), (8, 8), (half - 8, 8)):
                at = base + (start_dir + start) * 8 + row
                send_rows[side, chunk, fi * half + start:fi * half + start + count, :] = spec[
                    pl.ds(at, count, stride=8), :
                ]

    for f in range(freqs):
        pack_freq(f, f // per_chunk, f % per_chunk)

    def pack_group(g, _):
        def one(m, accs):
            f = jnp.minimum(g * per_group + m, freqs - 1)
            base = f * (dirs * 8)
            out = []
            for side, chosen, extra in ((0, east_dirs, 1), (1, west_dirs, 0)):
                acc = jnp.zeros((8, 128), f32)
                for j, d in enumerate(chosen):
                    tile = spec[pl.ds(pl.multiple_of(base + d * 8, 8), 8), :]
                    acc = jnp.where(lane == j, roll(tile, j + extra, 1), acc)
                acc = pltpu.roll(acc, half * m, 1)
                here = (lane >= half * m) & (lane < half * m + half)
                out.append(jnp.where(here, acc, accs[side]))
            return tuple(out)

        zero = jnp.zeros((8, 128), f32)
        a, b = lax.fori_loop(0, per_group, one, (zero, zero))
        send_cols[0, g] = a
        send_cols[1, g] = b
        return 0

    lax.fori_loop(0, groups, pack_group, 0)

    for copy in loads[4:]:
        copy.wait()
    for d in range(dirs):
        table[0, d] = abs(cosines[d])
        table[1, d] = abs(sines[d])
    group = 3

    def weigh(step, _):
        total = [[jnp.zeros((8, 128), f32)] * 4 for _ in range(group)]
        for f in range(freqs):
            a, b, c = stokes[f], stress[f], courant[f]
            ws = [jnp.full((8, 128), w, f32) for w in (a, b, a * c, b * c)]
            for n in range(group):
                at = f * dirs * 8 + (step * group + n) * 8
                tile = spec[pl.ds(pl.multiple_of(at, 8), 8), :]
                total[n] = [t + w * tile for t, w in zip(total[n], ws)]
        for n in range(group):
            for i in range(4):
                acc[i, step * group + n] = total[n][i]
        return 0

    lax.fori_loop(0, dirs // group, weigh, 0)

    zero = jnp.zeros((8, 128), f32)
    bases = [
        (c, s, c * c, c * s, s * s) for c, s in zip(cosines, sines)
    ]
    north, south, east, west = [], [], [], []
    for w in range(2):
        mid = [zero] * 5
        ns = [[zero] * 5, [zero] * 5]
        ew = [[zero] * 5, [zero] * 5]
        for d in range(dirs):
            plain, moved = acc[w, d], acc[2 + w, d]
            along_x, along_y = abs(cosines[d]), abs(sines[d])
            kept = plain - (along_x + along_y) * moved
            to_x, to_y = along_x * moved, along_y * moved
            x, y = 0 if cosines[d] > 0 else 1, 0 if sines[d] > 0 else 1
            for m in range(5):
                mid[m] = mid[m] + bases[d][m] * kept
                ns[y][m] = ns[y][m] + bases[d][m] * to_y
                ew[x][m] = ew[x][m] + bases[d][m] * to_x
        for m in range(5):
            gsum[5 * w + m] = (
                mid[m]
                + jnp.where(sub > 0, roll(ns[0][m], 1, 0), 0.0)
                + jnp.where(sub < 7, roll(ns[1][m], -1, 0), 0.0)
                + jnp.where(lane > 0, roll(ew[0][m], 1, 1), 0.0)
                + jnp.where(lane < 127, roll(ew[1][m], -1, 1), 0.0)
            )
            for i, out in enumerate((ns[0][m], ns[1][m], ew[0][m], ew[1][m])):
                sums[i, 5 * w + m] = out

    for g in range(n_sum):
        hrow[0, g:g + 1, :] = sums[0, g, 7:8, :]
        hrow[1, g:g + 1, :] = sums[1, g, 0:1, :]
    to_east, to_west = zero, zero
    for g in range(n_sum):
        to_east = jnp.where(lane == g, roll(sums[2, g], g - 127, 1), to_east)
        to_west = jnp.where(lane == g, roll(sums[3, g], g, 1), to_west)
    hcol[0] = to_east
    hcol[1] = to_west

    def pack_rows(tiles, ref):
        for p in range(len(tiles) // 2):
            a, b = tiles[2 * p], tiles[2 * p + 1]
            ref[0, p] = jnp.where(sub >= 4, b, roll(a, 4, 0))
            ref[1, p] = jnp.where(sub < 4, a, roll(b, 4, 0))

    def pack_cols(tiles, ref):
        to_east = jnp.zeros((8, 128), f32)
        to_west = jnp.zeros((8, 128), f32)
        for i, tile in enumerate(tiles):
            here = (lane >= 4 * i) & (lane < 4 * i + 4)
            to_east = jnp.where(here, roll(tile, 4 * i + 4, 1), to_east)
            to_west = jnp.where(here, roll(tile, 4 * i, 1), to_west)
        ref[0] = to_east
        ref[1] = to_west

    plain = [own[q * levels + p] for q in range(2) for p in range(1, levels)]
    n_near = len(plain)
    tiles = plain + [own[0], own[levels], edges[0], edges[1]]
    pack_rows(tiles, rowpk)
    pack_cols(tiles, colpk)

    edge = jnp.where(north_ok, 0, 3) + jnp.where(south_ok, 0, 3)
    pl.semaphore_wait(barrier, 9 - edge)
    for ds, dy, dx in partners:
        if ds == 0:
            def say(dy=dy, dx=dx):
                pl.semaphore_signal(ready, inc=1, device_id=target(0, dy, dx), device_id_type=MESH)
            when_to(dy, say)

    messages = []

    def message(src, dst, ds, dy, dx):
        messages.append((src, dst, ds, dy, dx))
        return len(messages) - 1

    def make(i):
        src, dst, ds, dy, dx = messages[i]
        return pltpu.make_async_remote_copy(
            src_ref=src, dst_ref=dst, send_sem=send_sem.at[i], recv_sem=recv_sem.at[i],
            device_id=target(ds, dy, dx), device_id_type=MESH,
        )

    def start(i):
        when_to(messages[i][3], lambda: make(i).start())

    def wait_recv(i):
        when_to(-messages[i][3], lambda: make(i).wait_recv())

    def wait_send(i):
        when_to(messages[i][3], lambda: make(i).wait_send())

    center = message(own, oth, 1, 0, 0)
    rim_sums = [message(hrow.at[s], hrow_in.at[s], 0, 1 - 2 * s, 0) for s in range(2)]
    rim_sums += [message(hcol.at[s], hcol_in.at[s], 0, 0, 1 - 2 * s) for s in range(2)]
    cols = [message(send_cols.at[s], recv_cols.at[s], 0, 0, 1 - 2 * s) for s in range(2)]
    rows = [
        [message(send_rows.at[s, c], recv_rows.at[s, c], 0, 1 - 2 * s, 0) for s in range(2)]
        for c in range(CHUNKS)
    ]

    def edge_messages(ds, row_src, row_dst, col_src, col_dst, count):
        out = []
        for dy in (-1, 1, 0):
            for s in range(2):
                out.append(message(col_src.at[s], col_dst.at[ds, 1 + dy, s], ds, dy, 1 - 2 * s))
        for s in range(2):
            out.append(
                message(row_src.at[s, 0:count], row_dst.at[ds, s, 0:count], ds, 1 - 2 * s, 0)
            )
        return out

    field_edges = edge_messages(0, rowpk, row_in, colpk, col_in, (2 * levels + 2) // 2)
    for i in [center] + rim_sums + cols + sum(rows, []) + field_edges:
        start(i)

    @pl.when(jnp.logical_not(south_ok))
    def _():
        recv_rows[0] = jnp.zeros(recv_rows.shape[1:], f32)
        hrow_in[0] = jnp.zeros(hrow_in.shape[1:], f32)

    @pl.when(jnp.logical_not(north_ok))
    def _():
        recv_rows[1] = jnp.zeros(recv_rows.shape[1:], f32)
        hrow_in[1] = jnp.zeros(hrow_in.shape[1:], f32)

    for i in rim_sums:
        wait_recv(i)
    full = []
    for g in range(n_sum):
        full.append(
            gsum[g]
            + jnp.where(sub == 0, hrow_in[0, g:g + 1, :], 0.0)
            + jnp.where(sub == 7, hrow_in[1, g:g + 1, :], 0.0)
            + jnp.where(lane == 0, roll(hcol_in[0], -g, 1), 0.0)
            + jnp.where(lane == 127, roll(hcol_in[1], 127 - g, 1), 0.0)
        )
    pl.semaphore_wait(ready, 8 - edge)
    cross = edge_messages(1, rowpk, row_in, colpk, col_in, n_near // 2)
    for i in cross:
        start(i)
    field_edges += cross

    wait_recv(center)
    su = jnp.where(first, own[0], oth[0])
    sv = jnp.where(first, own[levels], oth[levels])
    parts = []
    for w in range(2):
        c, s, cc, cs, ss = full[5 * w:5 * w + 5]
        parts.append(sea * (c + CURRENT_GAIN * (su * cc + sv * cs)))
        parts.append(sea * (s + CURRENT_GAIN * (su * cs + sv * ss)))

    for i in range(4):
        cpl[i] = parts[i]
    pack_rows(parts, rowc)
    pack_cols(parts, colc)
    coupling = []
    coupling += edge_messages(1, rowc, rowc_in, colc, colc_in, 2)
    coupling += [message(cpl, cplo, 1, 0, 0)]
    coupling += edge_messages(0, rowc, rowc_in, colc, colc_in, 2)
    for i in coupling:
        start(i)

    for d in range(dirs):
        dop[d] = sea * (1.0 + CURRENT_GAIN * (su * cosines[d] + sv * sines[d]))
    for i in cols:
        wait_recv(i)

    def wave(chunk, fi, _):
        f = chunk * per_chunk + fi
        base = f * (dirs * 8)
        speed = jnp.full((8, 128), courant[f], f32)
        g = f // per_group
        m = f - g * per_group
        back = lax.rem(128 - half * m, 128)
        from_west = pltpu.roll(recv_cols[0, g], back, 1)
        from_east = pltpu.roll(recv_cols[1, g], back, 1)
        for d in range(dirs):
            at = pl.ds(pl.multiple_of(base + d * 8, 8), 8)
            tile = spec[at, :]
            if cosines[d] > 0:
                j = east_dirs.index(d)
                beside = jnp.where(lane == 0, roll(from_west, -j, 1), roll(tile, 1, 1))
            else:
                j = west_dirs.index(d)
                beside = jnp.where(lane == 127, roll(from_east, 127 - j, 1), roll(tile, -1, 1))
            if sines[d] > 0:
                row = recv_rows[0, chunk, pl.ds(fi * half + north_dirs.index(d), 1), :]
                along = jnp.where(sub == 0, row, roll(tile, 1, 0))
            else:
                row = recv_rows[1, chunk, pl.ds(fi * half + south_dirs.index(d), 1), :]
                along = jnp.where(sub == 7, row, roll(tile, -1, 0))
            change = abs(cosines[d]) * (beside - tile) + abs(sines[d]) * (along - tile)
            out_spec[at, :] = (tile + speed * change) * dop[d]
        return 0

    for c in range(CHUNKS):
        for i in rows[c]:
            wait_recv(i)
        lax.fori_loop(0, per_chunk, functools.partial(wave, c), 0)

    inside = jnp.where(sub < 4, north_ok.astype(jnp.int32), south_ok.astype(jnp.int32)) != 0
    zero = jnp.zeros((8, 128), f32)

    def ghost_rows(from_south, from_north, i):
        p = i // 2
        if i % 2 == 0:
            low, high = roll(from_south[p], 4, 0), from_north[p]
        else:
            low, high = from_south[p], roll(from_north[p], 4, 0)
        return jnp.where(inside, jnp.where(sub < 4, high, low), zero)

    def ghost_lanes(from_west, from_east, i):
        return jnp.where(
            lane < 4,
            roll(from_east, -4 * i, 1),
            jnp.where(lane >= 124, roll(from_west, 124 - 4 * i, 1), zero),
        )

    for i in field_edges:
        wait_recv(i)

    def packs(rows_in, cols_in, r, count):
        from_south = [rows_in[r, 0, p] for p in range(count // 2)]
        from_north = [rows_in[r, 1, p] for p in range(count // 2)]
        side = [cols_in[r, 1, s] for s in range(2)]
        corner = [
            jnp.where(inside, jnp.where(sub < 4, cols_in[r, 0, s], cols_in[r, 2, s]), zero)
            for s in range(2)
        ]
        return from_south, from_north, side, corner

    def place(ref, index, own, got, i):
        from_south, from_north, side, corner = got
        ref[index + (slice(0, 8), slice(0, 128))] = own
        ref[index + (slice(0, 8), slice(128, 256))] = ghost_lanes(side[0], side[1], i)
        ref[index + (slice(8, 16), slice(0, 128))] = ghost_rows(from_south, from_north, i)
        ref[index + (slice(8, 16), slice(128, 256))] = ghost_lanes(corner[0], corner[1], i)

    for r in range(2):
        got = packs(row_in, col_in, r, 2 * levels + 2 if r == 0 else n_near)
        for q in range(2):
            for p in range(levels):
                tile = (own if r == 0 else oth)[q * levels + p]
                at = (q, p if r == 0 else 2 * levels - 1 - p)
                if p > 0:
                    place(ext, at, tile, got, q * (levels - 1) + p - 1)
                elif r == 0:
                    place(ext, at, tile, got, n_near + q)
                else:
                    ext[at] = jnp.zeros((16, 256), f32)
                    ext[at + (slice(0, 8), slice(0, 128))] = tile
        if r == 0:
            for n in range(2):
                place(aux, (n,), edges[n], got, n_near + 2 + n)

    big_sub = lax.broadcasted_iota(jnp.int32, (16, 256), 0)
    row_index = jnp.where(big_sub < 12, big_sub, big_sub - 16) + lat * 8
    aux[2] = 0.05 + 0.1 * (row_index.astype(f32) + 0.5) / (8 * lats)

    total = 2 * levels

    def at_level(p, _):
        ocean_level(ext, ext2, aux, None, first, total, p)
        return 0

    ocean_level(ext, ext2, aux, None, first, total, 0)
    lax.fori_loop(1, total - 1, at_level, 0)

    for i in coupling:
        wait_recv(i)
    got = [packs(rowc_in, colc_in, r, 4) for r in range(2)]
    both = jax.tree.map(lambda a, b: a + b, got[0], got[1])
    for i in range(4):
        place(frc, (i,), cpl[i] + cplo[i], both, i)
    for i in range(len(messages)):
        wait_send(i)


def level_of(first, total, p):
    return jnp.where(first, p, total - 1 - p)


def forcing(aux, frc, first, total, p):
    k = level_of(first, total, p)
    decay = aux[2] / (1.0 + k.astype(f32))
    top = jnp.where(k == 0, STRESS_GAIN, 0.0)
    return decay * frc[1] + top * frc[2], top * frc[3] - decay * frc[0]


def ocean_level(src, dst, aux, frc, first, total, p):
    k = level_of(first, total, p)
    mix = 0.04 + 0.0125 * lax.rem(7 * k, 5).astype(f32)
    center = [src[0, p], src[1, p]]
    new = []
    for q in range(2):
        mid = center[q]
        lap = (
            roll(mid, -1, 0) + roll(mid, 1, 0) + roll(mid, -1, 1) + roll(mid, 1, 1) - 4.0 * mid
        )
        vert = src[q, p + 1] - mid
        if not (isinstance(p, int) and p == 0):
            vert = vert + (src[q, p - 1] - mid)
        new.append(mid + aux[1] * lap + mix * vert)
    new[0] = new[0] + aux[2] * center[1]
    new[1] = new[1] - aux[2] * center[0]
    if frc is not None:
        force = forcing(aux, frc, first, total, p)
        new = [new[0] + force[0], new[1] + force[1]]
    for q in range(2):
        if dst.shape[-1] == 256:
            dst[q, p] = aux[0] * new[q]
        else:
            own = jnp.where(first, p, dst.shape[1] - 1 - p)
            dst[q, own] = (aux[0] * new[q])[0:8, 0:128]


def emit(levels, spec, ext2, aux, frc, out_spec, out_cur, fa, fb, cur, sems):
    part = spec.shape[0] // EMIT
    copies = []
    for i in range(EMIT):
        at = pl.ds(i * part, part)
        copies.append(pltpu.make_async_copy(spec.at[at], out_spec.at[at], sems.at[i]))
    for copy in copies:
        copy.start()
    first = lax.axis_index("sec") == 0
    total = 2 * levels
    for p in range(total - 1):
        force = forcing(aux, frc, first, total, p)
        for q in range(2):
            fa[q, p] = ext2[q, p] + aux[0] * force[q]
    src, dst = fa, fb
    for step in range(1, ITERS):
        for p in range(total - 1 - step):
            ocean_level(src, cur if step == ITERS - 1 else dst, aux, frc, first, total, p)
        src, dst = dst, src
    last = pltpu.make_async_copy(cur, out_cur, sems.at[EMIT])
    last.start()
    for copy in copies:
        copy.wait()
    last.wait()


def shards(lats, lons, spectra, currents, land_mask, diffusion, courant, stokes_weight, stress_weight):
    freqs, dirs, tile_rows, tile_cols = spectra.shape
    levels = currents.shape[1]
    cells = freqs * dirs * tile_rows
    half = dirs // 2
    rows = -(-freqs // CHUNKS * half // 8) * 8
    groups = -(-freqs // (128 // half))
    tile = (8, 128)
    vmem = lambda *shape: pltpu.VMEM(shape, f32)
    any_spec = pl.BlockSpec(memory_space=pl.ANY)
    n_msg = 7 + 2 * CHUNKS + 16 + 17
    big = (2, 2 * levels, 16, 256)
    vmem_spec = pl.BlockSpec(memory_space=pltpu.VMEM)
    results = pl.pallas_call(
        functools.partial(kernel, freqs, dirs, levels, lats, lons),
        out_shape=(vmem(cells, 128), vmem(*big), vmem(3, 16, 256), vmem(4, 16, 256)),
        in_specs=[any_spec] * 7,
        out_specs=(vmem_spec,) * 4,
        scratch_shapes=[
            vmem(cells, 128), vmem(2, levels, *tile),
            pltpu.VMEM(tile, jnp.int32), vmem(*tile),
            pltpu.SMEM((freqs,), f32), pltpu.SMEM((freqs,), f32), pltpu.SMEM((freqs,), f32),
            pltpu.SMEM((2, dirs), f32),
            vmem(2, CHUNKS, rows, 128), vmem(2, CHUNKS, rows, 128),
            vmem(2, groups, *tile), vmem(2, groups, *tile),
            vmem(2 * levels, *tile), vmem(2 * levels, *tile), vmem(2, *tile),
            vmem(2, levels + 1, *tile), vmem(2, 2, levels + 1, *tile),
            vmem(2, *tile), vmem(2, 3, 2, *tile),
            vmem(4, *tile), vmem(4, *tile),
            vmem(2, 2, *tile), vmem(2, 2, 2, *tile),
            vmem(2, *tile), vmem(2, 3, 2, *tile),
            vmem(dirs, *tile), vmem(4, dirs, *tile), vmem(10, *tile), vmem(4, 10, *tile),
            vmem(2, 16, 128), vmem(2, 16, 128), vmem(2, *tile), vmem(2, *tile), vmem(*big),
            pltpu.SemaphoreType.DMA((7,)),
            pltpu.SemaphoreType.DMA((n_msg,)),
            pltpu.SemaphoreType.DMA((n_msg,)),
            pltpu.SemaphoreType.REGULAR,
        ],
        compiler_params=pltpu.CompilerParams(collective_id=0, has_side_effects=True),
        name="window",
    )(spectra.reshape(cells, tile_cols), currents, land_mask, diffusion, courant, stokes_weight, stress_weight)
    results = [pltpu.with_memory_space_constraint(r, pltpu.VMEM) for r in results]
    new_spectra, new_currents = pl.pallas_call(
        functools.partial(emit, levels),
        out_shape=(
            jax.ShapeDtypeStruct((cells, tile_cols), f32),
            jax.ShapeDtypeStruct(currents.shape, f32),
        ),
        in_specs=[vmem_spec] * 4,
        out_specs=(any_spec, any_spec),
        scratch_shapes=[
            vmem(*big), vmem(*big), vmem(2, levels, *tile), pltpu.SemaphoreType.DMA((EMIT + 1,)),
        ],
        name="emit",
    )(*results)
    return new_spectra.reshape(spectra.shape), new_currents


def solution(mesh):
    in_specs = (
        P("sec", None, "lat", "lon"),
        P(None, "sec", "lat", "lon"),
        P("lat", "lon"),
        P("lat", "lon"),
        P("sec"),
        P("sec"),
        P("sec"),
    )
    out_specs = (P("sec", None, "lat", "lon"), P(None, "sec", "lat", "lon"))
    body = functools.partial(shards, mesh.shape["lat"], mesh.shape["lon"])
    return jax.shard_map(body, mesh=mesh, in_specs=in_specs, out_specs=out_specs, check_vma=False)
```

```python
import functools
import math

import jax
import jax.numpy as jnp
import numpy as np
from jax import lax
from jax.experimental import pallas as pl
from jax.experimental.pallas import tpu as pltpu
from jax.sharding import PartitionSpec as P

ITERS = 4
CURRENT_GAIN = 0.1
STRESS_GAIN = 0.5
MESH = pl.DeviceIdType.MESH
f32 = jnp.float32
CHUNKS = 3
EMIT = 4


def headings(directions):
    heading = ((np.arange(directions).astype(np.float32) + np.float32(0.5))
               * np.float32(2.0 * math.pi / directions)).astype(np.float64)
    return [float(np.float32(c)) for c in np.cos(heading)], [float(np.float32(s)) for s in np.sin(heading)]


def roll(x, shift, axis):
    shift = shift % x.shape[axis]
    return x if shift == 0 else pltpu.roll(x, shift, axis)


def kernel(
    freqs, dirs, levels, lats, lons,
    spec_hbm, cur_hbm, mask_hbm, diff_hbm, courant_hbm, stokes_hbm, stress_hbm,
    out_spec, ext, aux, frc,
    spec, curv, maskv, diffv, courant, stokes, stress, table,
    send_rows, recv_rows, send_cols, recv_cols,
    own, oth, edges, rowpk, row_in, colpk, col_in,
    pos, pos_in, rowc, rowc_in, colc, colc_in,
    dop, acc, sums,
    local_sem, send_sem, recv_sem,
):
    sec, lat, lon = lax.axis_index("sec"), lax.axis_index("lat"), lax.axis_index("lon")
    north_ok, south_ok = lat < lats - 1, lat > 0
    cosines, sines = headings(dirs)
    east_dirs = [d for d in range(dirs) if cosines[d] > 0]
    west_dirs = [d for d in range(dirs) if cosines[d] <= 0]
    north_dirs = [d for d in range(dirs) if sines[d] > 0]
    south_dirs = [d for d in range(dirs) if sines[d] <= 0]
    half = dirs // 2
    per_chunk = freqs // CHUNKS
    per_group = 128 // half
    groups = -(-freqs // per_group)

    def target(dsec, dlat, dlon):
        return (
            lax.rem(sec + dsec, 2),
            lat + dlat,
            lax.rem(lon + dlon + lons, lons),
        )

    def when_to(dlat, fn):
        if dlat == 0:
            fn()
        else:
            pl.when(north_ok if dlat > 0 else south_ok)(fn)

    partners = [
        (ds, dy, dx) for ds in (0, 1) for dy in (-1, 0, 1) for dx in (-1, 0, 1)
        if (ds, dy, dx) == (1, 0, 0) or (ds == 0 and (dy, dx) != (0, 0))
    ]
    loads = [
        pltpu.make_async_copy(cur_hbm, curv, local_sem.at[0]),
        pltpu.make_async_copy(mask_hbm, maskv, local_sem.at[1]),
        pltpu.make_async_copy(diff_hbm, diffv, local_sem.at[2]),
        pltpu.make_async_copy(spec_hbm, spec, local_sem.at[3]),
        pltpu.make_async_copy(courant_hbm, courant, local_sem.at[4]),
        pltpu.make_async_copy(stokes_hbm, stokes, local_sem.at[5]),
        pltpu.make_async_copy(stress_hbm, stress, local_sem.at[6]),
    ]
    for copy in loads:
        copy.start()
    barrier = pltpu.get_barrier_semaphore()
    for ds, dy, dx in partners:
        def greet(ds=ds, dy=dy, dx=dx):
            pl.semaphore_signal(barrier, inc=1, device_id=target(ds, dy, dx), device_id_type=MESH)
        when_to(dy, greet)

    lane = lax.broadcasted_iota(jnp.int32, (8, 128), 1)
    sub = lax.broadcasted_iota(jnp.int32, (8, 128), 0)

    first = sec == 0
    for copy in loads[:3]:
        copy.wait()
    sea = maskv[...].astype(f32)
    for q in range(2):
        for p in range(levels):
            own[q * levels + p] = curv[q, jnp.where(first, p, levels - 1 - p)] * sea
    edges[0] = sea
    edges[1] = diffv[...]
    n_fld, n_sum = 2 * levels, 10

    loads[3].wait()

    def pack_freq(f, chunk, fi):
        base = f * (dirs * 8)
        for side, start_dir, row in ((0, north_dirs[0], 7), (1, south_dirs[0], 0)):
            for start, count in ((0, 8), (8, 8), (half - 8, 8)):
                at = base + (start_dir + start) * 8 + row
                send_rows[side, chunk, fi * half + start:fi * half + start + count, :] = spec[
                    pl.ds(at, count, stride=8), :
                ]

    for f in range(freqs):
        pack_freq(f, f // per_chunk, f % per_chunk)

    def pack_group(g, _):
        def one(m, accs):
            f = jnp.minimum(g * per_group + m, freqs - 1)
            base = f * (dirs * 8)
            out = []
            for side, chosen, extra in ((0, east_dirs, 1), (1, west_dirs, 0)):
                acc = jnp.zeros((8, 128), f32)
                for j, d in enumerate(chosen):
                    tile = spec[pl.ds(pl.multiple_of(base + d * 8, 8), 8), :]
                    acc = jnp.where(lane == j, roll(tile, j + extra, 1), acc)
                acc = pltpu.roll(acc, half * m, 1)
                here = (lane >= half * m) & (lane < half * m + half)
                out.append(jnp.where(here, acc, accs[side]))
            return tuple(out)

        zero = jnp.zeros((8, 128), f32)
        a, b = lax.fori_loop(0, per_group, one, (zero, zero))
        send_cols[0, g] = a
        send_cols[1, g] = b
        return 0

    lax.fori_loop(0, groups, pack_group, 0)

    for copy in loads[4:]:
        copy.wait()
    for d in range(dirs):
        table[0, d] = abs(cosines[d])
        table[1, d] = abs(sines[d])
    group = 3

    def weigh(step, _):
        total = [[jnp.zeros((8, 128), f32)] * 4 for _ in range(group)]
        for f in range(freqs):
            a, b, c = stokes[f], stress[f], courant[f]
            ws = [jnp.full((8, 128), w, f32) for w in (a, b, a * c, b * c)]
            for n in range(group):
                at = f * dirs * 8 + (step * group + n) * 8
                tile = spec[pl.ds(pl.multiple_of(at, 8), 8), :]
                total[n] = [t + w * tile for t, w in zip(total[n], ws)]
        for n in range(group):
            for i in range(4):
                acc[i, step * group + n] = total[n][i]
        return 0

    lax.fori_loop(0, dirs // group, weigh, 0)

    zero = jnp.zeros((8, 128), f32)
    bases = [
        (c, s, c * c, c * s, s * s) for c, s in zip(cosines, sines)
    ]
    north, south, east, west = [], [], [], []
    for w in range(2):
        mid = [zero] * 5
        ns = [[zero] * 5, [zero] * 5]
        ew = [[zero] * 5, [zero] * 5]
        for d in range(dirs):
            plain, moved = acc[w, d], acc[2 + w, d]
            along_x, along_y = abs(cosines[d]), abs(sines[d])
            kept = plain - (along_x + along_y) * moved
            to_x, to_y = along_x * moved, along_y * moved
            x, y = 0 if cosines[d] > 0 else 1, 0 if sines[d] > 0 else 1
            for m in range(5):
                mid[m] = mid[m] + bases[d][m] * kept
                ns[y][m] = ns[y][m] + bases[d][m] * to_y
                ew[x][m] = ew[x][m] + bases[d][m] * to_x
        for m in range(5):
            pos[5 * w + m] = (
                mid[m]
                + jnp.where(sub > 0, roll(ns[0][m], 1, 0), 0.0)
                + jnp.where(sub < 7, roll(ns[1][m], -1, 0), 0.0)
                + jnp.where(lane > 0, roll(ew[0][m], 1, 1), 0.0)
                + jnp.where(lane < 127, roll(ew[1][m], -1, 1), 0.0)
            )
            for i, out in enumerate((ns[0][m], ns[1][m], ew[0][m], ew[1][m])):
                sums[i, 5 * w + m] = out

    rims_e_w = zero
    for g in range(n_sum):
        for side, row in ((0, 7), (1, 0)):
            at = 2 * g + side
            pos[n_sum + at // 8, at % 8:at % 8 + 1, :] = sums[side, g, row:row + 1, :]
        rims_e_w = jnp.where(lane == g, roll(sums[2, g], g - 127, 1), rims_e_w)
        rims_e_w = jnp.where(lane == n_sum + g, roll(sums[3, g], n_sum + g, 1), rims_e_w)
    n_pos = n_sum + -(-2 * n_sum // 8)
    pos[n_pos] = rims_e_w

    def pack_rows(tiles, ref):
        for p in range(len(tiles) // 2):
            (a_up, a_down), (b_up, b_down) = tiles[2 * p], tiles[2 * p + 1]
            ref[0, p] = jnp.where(sub >= 4, b_up, roll(a_up, 4, 0))
            ref[1, p] = jnp.where(sub < 4, a_down, roll(b_down, 4, 0))

    def pack_cols(tiles, ref):
        to_east, to_west = zero, zero
        for i, (te, tw) in enumerate(tiles):
            here = (lane >= 4 * i) & (lane < 4 * i + 4)
            to_east = jnp.where(here, roll(te, 4 * i + 4, 1), to_east)
            to_west = jnp.where(here, roll(tw, 4 * i, 1), to_west)
        ref[0] = to_east
        ref[1] = to_west

    same = [(t, t) for t in [own[i] for i in range(n_fld)] + [edges[0], edges[1]]]
    pack_rows(same, rowpk)
    pack_cols(same, colpk)

    edge = jnp.where(north_ok, 0, 3) + jnp.where(south_ok, 0, 3)
    pl.semaphore_wait(barrier, 9 - edge)

    messages = []

    def message(src, dst, ds, dy, dx):
        messages.append((src, dst, ds, dy, dx))
        return len(messages) - 1

    def make(i):
        src, dst, ds, dy, dx = messages[i]
        return pltpu.make_async_remote_copy(
            src_ref=src, dst_ref=dst, send_sem=send_sem.at[i], recv_sem=recv_sem.at[i],
            device_id=target(ds, dy, dx), device_id_type=MESH,
        )

    def start(i):
        when_to(messages[i][3], lambda: make(i).start())

    def wait_recv(i):
        when_to(-messages[i][3], lambda: make(i).wait_recv())

    def wait_send(i):
        when_to(messages[i][3], lambda: make(i).wait_send())

    center = [message(pos, pos_in, 1, 0, 0), message(own, oth, 1, 0, 0)]
    cols = [message(send_cols.at[s], recv_cols.at[s], 0, 0, 1 - 2 * s) for s in range(2)]
    rows = [
        [message(send_rows.at[s, c], recv_rows.at[s, c], 0, 1 - 2 * s, 0) for s in range(2)]
        for c in range(CHUNKS)
    ]

    def edge_messages(row_src, row_dst, col_src, col_dst):
        out = []
        for dy in (-1, 1, 0):
            for s in range(2):
                out.append(message(col_src(dy).at[s], col_dst.at[1 + dy, s], 0, dy, 1 - 2 * s))
        for s in range(2):
            out.append(message(row_src.at[s], row_dst.at[s], 0, 1 - 2 * s, 0))
        return out

    field_edges = edge_messages(rowpk, row_in, lambda dy: colpk, col_in)
    for i in center + cols + sum(rows, []) + field_edges:
        start(i)

    @pl.when(jnp.logical_not(south_ok))
    def _():
        recv_rows[0] = jnp.zeros(recv_rows.shape[1:], f32)
        for rows_in, cols_in in ((row_in, col_in), (rowc_in, colc_in)):
            rows_in[0] = jnp.zeros(rows_in.shape[1:], f32)
            cols_in[2] = jnp.zeros(cols_in.shape[1:], f32)

    @pl.when(jnp.logical_not(north_ok))
    def _():
        recv_rows[1] = jnp.zeros(recv_rows.shape[1:], f32)
        for rows_in, cols_in in ((row_in, col_in), (rowc_in, colc_in)):
            rows_in[1] = jnp.zeros(rows_in.shape[1:], f32)
            cols_in[0] = jnp.zeros(cols_in.shape[1:], f32)

    for i in cols:
        wait_recv(i)

    def wave(chunk, fi, _):
        f = chunk * per_chunk + fi
        base = f * (dirs * 8)
        speed = jnp.full((8, 128), courant[f], f32)
        g = f // per_group
        m = f - g * per_group
        back = lax.rem(128 - half * m, 128)
        from_west = pltpu.roll(recv_cols[0, g], back, 1)
        from_east = pltpu.roll(recv_cols[1, g], back, 1)
        for d in range(dirs):
            at = pl.ds(pl.multiple_of(base + d * 8, 8), 8)
            tile = spec[at, :]
            if cosines[d] > 0:
                j = east_dirs.index(d)
                beside = jnp.where(lane == 0, roll(from_west, -j, 1), roll(tile, 1, 1))
            else:
                j = west_dirs.index(d)
                beside = jnp.where(lane == 127, roll(from_east, 127 - j, 1), roll(tile, -1, 1))
            if sines[d] > 0:
                row = recv_rows[0, chunk, pl.ds(fi * half + north_dirs.index(d), 1), :]
                along = jnp.where(sub == 0, row, roll(tile, 1, 0))
            else:
                row = recv_rows[1, chunk, pl.ds(fi * half + south_dirs.index(d), 1), :]
                along = jnp.where(sub == 7, row, roll(tile, -1, 0))
            change = abs(cosines[d]) * (beside - tile) + abs(sines[d]) * (along - tile)
            out_spec[at, :] = tile + speed * change
        return 0

    for c in range(CHUNKS):
        for i in rows[c]:
            wait_recv(i)
        if c < CHUNKS - 1:
            lax.fori_loop(0, per_chunk, functools.partial(wave, c), 0)

    for i in center:
        wait_recv(i)
    for i in range(n_pos + 1):
        pos_in[i] = pos_in[i] + pos[i]
    rims = pos_in[n_pos]

    def rim_row(g, side):
        at = 2 * g + side
        return pos_in[n_sum + at // 8, at % 8:at % 8 + 1, :]

    def rim_col(g, side, at):
        return roll(rims, at - n_sum * side - g, 1)

    packed = [(oth[i], oth[i]) for i in range(n_fld)]
    by_dy = {dy: list(packed) for dy in (-1, 0, 1)}
    for g in range(n_sum):
        tile = pos_in[g]
        to_e, to_w = rim_col(g, 0, 127), rim_col(g, 1, 0)
        up = jnp.where(sub == 7, rim_row(g, 0), roll(tile, -1, 0))
        down = jnp.where(sub == 0, rim_row(g, 1), roll(tile, 1, 0))
        packed.append((up, down))
        pick = lambda t, e, w: (
            jnp.where(lane == 127, e, roll(t, -1, 1)), jnp.where(lane == 0, w, roll(t, 1, 1))
        )
        by_dy[0].append(pick(tile, to_e, to_w))
        by_dy[1].append(pick(up, *(jnp.where(sub == 7, 0.0, roll(t, -1, 0)) for t in (to_e, to_w))))
        by_dy[-1].append(pick(down, *(jnp.where(sub == 0, 0.0, roll(t, 1, 0)) for t in (to_e, to_w))))
    pack_rows(packed, rowc)
    for s in range(2):
        rowc[s, len(packed) // 2] = rims
    for g in range(n_sum):
        tile = jnp.where(sub == 7, rim_row(g, 0), jnp.where(sub == 0, rim_row(g, 1), 0.0))
        by_dy[0].append((roll(tile, -1, 1), roll(tile, 1, 1)))
    for dy in by_dy:
        pack_cols(by_dy[dy], colc.at[1 + dy])
    sum_edges = edge_messages(rowc, rowc_in, lambda dy: colc.at[1 + dy], colc_in)
    for i in sum_edges:
        start(i)

    lax.fori_loop(0, per_chunk, functools.partial(wave, CHUNKS - 1), 0)
    su = jnp.where(first, own[0], oth[0])
    sv = jnp.where(first, own[levels], oth[levels])
    for d in range(dirs):
        dop[d] = sea * (1.0 + CURRENT_GAIN * (su * cosines[d] + sv * sines[d]))

    def scale(f, _):
        for d in range(dirs):
            at = pl.ds(pl.multiple_of(f * (dirs * 8) + d * 8, 8), 8)
            out_spec[at, :] = out_spec[at, :] * dop[d]
        return 0

    lax.fori_loop(0, freqs, scale, 0)

    for i in field_edges:
        wait_recv(i)

    def put(ref, index, quads):
        for n, (r, l) in enumerate(((0, 0), (0, 128), (8, 0), (8, 128))):
            ref[index + (slice(r, r + 8), slice(l, l + 128))] = quads[n]

    def ghosts(rows_in, cols_in, i):
        def lanes(dy):
            return jnp.where(
                lane < 4,
                roll(cols_in[1 + dy, 1], -4 * i, 1),
                jnp.where(lane >= 124, roll(cols_in[1 + dy, 0], 124 - 4 * i, 1), 0.0),
            )

        p = i // 2
        if i % 2 == 0:
            low, high = roll(rows_in[0, p], 4, 0), rows_in[1, p]
        else:
            low, high = rows_in[0, p], roll(rows_in[1, p], 4, 0)
        corner = jnp.where(sub < 4, lanes(-1), lanes(1))
        return lanes(0), jnp.where(sub < 4, high, low), corner

    for q in range(2):
        for p in range(levels):
            i = q * levels + p
            put(ext, (q, p), (own[i],) + ghosts(row_in, col_in, i))
    for n in range(2):
        put(aux, (n,), (edges[n],) + ghosts(row_in, col_in, n_fld + n))

    big_sub = lax.broadcasted_iota(jnp.int32, (16, 256), 0)
    row_index = jnp.where(big_sub < 12, big_sub, big_sub - 16) + lat * 8
    aux[2] = 0.05 + 0.1 * (row_index.astype(f32) + 0.5) / (8 * lats)

    for i in sum_edges:
        wait_recv(i)
    for q in range(2):
        for p in range(levels):
            i = q * levels + p
            put(ext, (q, 2 * levels - 1 - p), (oth[i],) + ghosts(rowc_in, colc_in, i))

    def lanes_of(dy, i):
        from_w = roll(colc_in[1 + dy, 0], 125 - 4 * i, 1)
        from_e = roll(colc_in[1 + dy, 1], -4 * i - 1, 1)
        inner = jnp.where(lane == 0, from_w, jnp.where(lane == 127, from_e, 0.0))
        outer = jnp.where(lane < 3, from_e, jnp.where(lane >= 125, from_w, 0.0))
        return inner, outer

    last = (n_fld + n_sum) // 2
    far_rims = jnp.where(sub < 3, rowc_in[1, last], jnp.where(sub >= 5, rowc_in[0, last], 0.0))
    total = []
    for g in range(n_sum):
        i = n_fld + g
        p = i // 2
        inner, outer = lanes_of(0, i)
        low = roll(rowc_in[0, p], 5 if i % 2 == 0 else 1, 0)
        high = roll(rowc_in[1, p], -1 if i % 2 == 0 else 3, 0)
        s_inner, s_outer = (roll(t, 1, 0) for t in lanes_of(1, i))
        n_inner, n_outer = (roll(t, -1, 0) for t in lanes_of(-1, i))
        low, high = low + s_inner, high + n_inner
        mine_out = jnp.where(
            lane == 0, rim_col(g, 0, 0), jnp.where(lane == 127, rim_col(g, 1, 127), 0.0)
        )
        mine_rows = jnp.where(sub == 0, rim_row(g, 0), jnp.where(sub == 7, rim_row(g, 1), 0.0))
        beside = lanes_of(0, n_fld + n_sum + g)[1]
        corner = jnp.where(
            sub == 0, roll(beside, 1, 0), jnp.where(sub == 7, roll(beside, -1, 0), 0.0)
        ) + jnp.where(
            lane == 0, roll(far_rims, -g, 1),
            jnp.where(lane == 127, roll(far_rims, 127 - n_sum - g, 1), 0.0),
        )
        edge_rows = lambda a, b: jnp.where(sub == 0, a, jnp.where(sub == 7, b, 0.0))
        out_rows = lambda a, b: jnp.where(sub < 3, b, jnp.where(sub >= 5, a, 0.0))
        total.append((
            pos_in[g] + inner + edge_rows(low, high),
            mine_out + outer + edge_rows(s_outer, n_outer),
            mine_rows + out_rows(low, high),
            corner + out_rows(s_outer, n_outer),
        ))
    surface_at = jnp.where(first, 0, 2 * levels - 1)
    for n, (r, l) in enumerate(((0, 0), (0, 128), (8, 0), (8, 128))):
        at = (slice(r, r + 8), slice(l, l + 128))
        su = CURRENT_GAIN * ext[(0, surface_at) + at]
        sv = CURRENT_GAIN * ext[(1, surface_at) + at]
        for w in range(2):
            c, s, cc, cs, ss = (total[5 * w + m][n] for m in range(5))
            frc[(2 * w,) + at] = aux[(0,) + at] * (c + su * cc + sv * cs)
            frc[(2 * w + 1,) + at] = aux[(0,) + at] * (s + su * cs + sv * ss)
    for i in range(len(messages)):
        wait_send(i)


def level_of(first, total, p):
    return jnp.where(first, p, total - 1 - p)


def forcing(aux, frc, first, total, p):
    k = level_of(first, total, p)
    decay = aux[2] / (1.0 + k.astype(f32))
    top = jnp.where(k == 0, STRESS_GAIN, 0.0)
    return decay * frc[1] + top * frc[2], top * frc[3] - decay * frc[0]


def ocean_level(src, dst, aux, frc, first, total, p):
    k = level_of(first, total, p)
    mix = 0.04 + 0.0125 * lax.rem(7 * k, 5).astype(f32)
    center = [src[0, p], src[1, p]]
    new = []
    for q in range(2):
        mid = center[q]
        lap = (
            roll(mid, -1, 0) + roll(mid, 1, 0) + roll(mid, -1, 1) + roll(mid, 1, 1) - 4.0 * mid
        )
        vert = src[q, p + 1] - mid
        if not (isinstance(p, int) and p == 0):
            vert = vert + (src[q, p - 1] - mid)
        new.append(mid + aux[1] * lap + mix * vert)
    new[0] = new[0] + aux[2] * center[1]
    new[1] = new[1] - aux[2] * center[0]
    if frc is not None:
        force = forcing(aux, frc, first, total, p)
        new = [new[0] + force[0], new[1] + force[1]]
    for q in range(2):
        if dst.shape[-1] == 256:
            dst[q, p] = aux[0] * new[q]
        else:
            own = jnp.where(first, p, dst.shape[1] - 1 - p)
            dst[q, own] = (aux[0] * new[q])[0:8, 0:128]


def emit(levels, spec, ext, aux, frc, out_spec, out_cur, fa, fb, cur, sems):
    part = spec.shape[0] // EMIT
    copies = []
    for i in range(EMIT):
        at = pl.ds(i * part, part)
        copies.append(pltpu.make_async_copy(spec.at[at], out_spec.at[at], sems.at[i]))
    for copy in copies:
        copy.start()
    first = lax.axis_index("sec") == 0
    total = 2 * levels
    src, dst = ext, fa
    for step in range(ITERS):
        for p in range(total - 1 - step):
            ocean_level(src, cur if step == ITERS - 1 else dst, aux, frc, first, total, p)
        src, dst = dst, fb if dst is fa else fa
    last = pltpu.make_async_copy(cur, out_cur, sems.at[EMIT])
    last.start()
    for copy in copies:
        copy.wait()
    last.wait()


def shards(lats, lons, spectra, currents, land_mask, diffusion, courant, stokes_weight, stress_weight):
    freqs, dirs, tile_rows, tile_cols = spectra.shape
    levels = currents.shape[1]
    cells = freqs * dirs * tile_rows
    half = dirs // 2
    rows = -(-freqs // CHUNKS * half // 8) * 8
    groups = -(-freqs // (128 // half))
    tile = (8, 128)
    vmem = lambda *shape: pltpu.VMEM(shape, f32)
    any_spec = pl.BlockSpec(memory_space=pl.ANY)
    n_msg = 4 + 2 * CHUNKS + 16
    big = (2, 2 * levels, 16, 256)
    vmem_spec = pl.BlockSpec(memory_space=pltpu.VMEM)
    results = pl.pallas_call(
        functools.partial(kernel, freqs, dirs, levels, lats, lons),
        out_shape=(vmem(cells, 128), vmem(*big), vmem(3, 16, 256), vmem(4, 16, 256)),
        in_specs=[any_spec] * 7,
        out_specs=(vmem_spec,) * 4,
        scratch_shapes=[
            vmem(cells, 128), vmem(2, levels, *tile),
            pltpu.VMEM(tile, jnp.int32), vmem(*tile),
            pltpu.SMEM((freqs,), f32), pltpu.SMEM((freqs,), f32), pltpu.SMEM((freqs,), f32),
            pltpu.SMEM((2, dirs), f32),
            vmem(2, CHUNKS, rows, 128), vmem(2, CHUNKS, rows, 128),
            vmem(2, groups, *tile), vmem(2, groups, *tile),
            vmem(2 * levels, *tile), vmem(2 * levels, *tile), vmem(2, *tile),
            vmem(2, levels + 1, *tile), vmem(2, levels + 1, *tile),
            vmem(2, *tile), vmem(3, 2, *tile),
            vmem(14, *tile), vmem(14, *tile),
            vmem(2, levels + 6, *tile), vmem(2, levels + 6, *tile),
            vmem(3, 2, *tile), vmem(3, 2, *tile),
            vmem(dirs, *tile), vmem(4, dirs, *tile), vmem(4, 10, *tile),
            pltpu.SemaphoreType.DMA((7,)),
            pltpu.SemaphoreType.DMA((n_msg,)),
            pltpu.SemaphoreType.DMA((n_msg,)),
        ],
        compiler_params=pltpu.CompilerParams(collective_id=0, has_side_effects=True),
        name="window",
    )(spectra.reshape(cells, tile_cols), currents, land_mask, diffusion, courant, stokes_weight, stress_weight)
    results = [pltpu.with_memory_space_constraint(r, pltpu.VMEM) for r in results]
    new_spectra, new_currents = pl.pallas_call(
        functools.partial(emit, levels),
        out_shape=(
            jax.ShapeDtypeStruct((cells, tile_cols), f32),
            jax.ShapeDtypeStruct(currents.shape, f32),
        ),
        in_specs=[vmem_spec] * 4,
        out_specs=(any_spec, any_spec),
        scratch_shapes=[
            vmem(*big), vmem(*big), vmem(2, levels, *tile), pltpu.SemaphoreType.DMA((EMIT + 1,)),
        ],
        name="emit",
    )(*results)
    return new_spectra.reshape(spectra.shape), new_currents


def solution(mesh):
    in_specs = (
        P("sec", None, "lat", "lon"),
        P(None, "sec", "lat", "lon"),
        P("lat", "lon"),
        P("lat", "lon"),
        P("sec"),
        P("sec"),
        P("sec"),
    )
    out_specs = (P("sec", None, "lat", "lon"), P(None, "sec", "lat", "lon"))
    body = functools.partial(shards, mesh.shape["lat"], mesh.shape["lon"])
    return jax.shard_map(body, mesh=mesh, in_specs=in_specs, out_specs=out_specs, check_vma=False)
```

```python
import functools
import math

import jax
import jax.numpy as jnp
import numpy as np
from jax import lax
from jax.experimental import pallas as pl
from jax.experimental.pallas import tpu as pltpu
from jax.sharding import PartitionSpec as P

ITERS = 4
CURRENT_GAIN = 0.1
STRESS_GAIN = 0.5
MESH = pl.DeviceIdType.MESH
f32 = jnp.float32
CHUNKS = 3
EMIT = 4


def headings(directions):
    heading = ((np.arange(directions).astype(np.float32) + np.float32(0.5))
               * np.float32(2.0 * math.pi / directions)).astype(np.float64)
    return [float(np.float32(c)) for c in np.cos(heading)], [float(np.float32(s)) for s in np.sin(heading)]


def roll(x, shift, axis):
    shift = shift % x.shape[axis]
    return x if shift == 0 else pltpu.roll(x, shift, axis)


def kernel(
    freqs, dirs, levels, lats, lons,
    spec_hbm, cur_hbm, mask_hbm, diff_hbm, courant_hbm, stokes_hbm, stress_hbm,
    out_spec, ext, aux, frc,
    spec, curv, maskv, diffv, courant, stokes, stress, table,
    send_rows, recv_rows, send_cols, recv_cols,
    own, oth, edges, rowpk, row_in, colpk, col_in,
    pos, pos_in, rowc, rowc_in, colc, colc_in, rowo, rowo_in, colo, colo_in,
    dop, acc, sums,
    local_sem, send_sem, recv_sem,
):
    sec, lat, lon = lax.axis_index("sec"), lax.axis_index("lat"), lax.axis_index("lon")
    north_ok, south_ok = lat < lats - 1, lat > 0
    cosines, sines = headings(dirs)
    east_dirs = [d for d in range(dirs) if cosines[d] > 0]
    west_dirs = [d for d in range(dirs) if cosines[d] <= 0]
    north_dirs = [d for d in range(dirs) if sines[d] > 0]
    south_dirs = [d for d in range(dirs) if sines[d] <= 0]
    half = dirs // 2
    per_chunk = freqs // CHUNKS
    per_group = 128 // half
    groups = -(-freqs // per_group)

    def target(dsec, dlat, dlon):
        return (
            lax.rem(sec + dsec, 2),
            lat + dlat,
            lax.rem(lon + dlon + lons, lons),
        )

    def when_to(dlat, fn):
        if dlat == 0:
            fn()
        else:
            pl.when(north_ok if dlat > 0 else south_ok)(fn)

    partners = [
        (ds, dy, dx) for ds in (0, 1) for dy in (-1, 0, 1) for dx in (-1, 0, 1)
        if (ds, dy, dx) == (1, 0, 0) or (ds == 0 and (dy, dx) != (0, 0))
    ]
    loads = [
        pltpu.make_async_copy(cur_hbm, curv, local_sem.at[0]),
        pltpu.make_async_copy(mask_hbm, maskv, local_sem.at[1]),
        pltpu.make_async_copy(diff_hbm, diffv, local_sem.at[2]),
        pltpu.make_async_copy(spec_hbm, spec, local_sem.at[3]),
        pltpu.make_async_copy(courant_hbm, courant, local_sem.at[4]),
        pltpu.make_async_copy(stokes_hbm, stokes, local_sem.at[5]),
        pltpu.make_async_copy(stress_hbm, stress, local_sem.at[6]),
    ]
    for copy in loads:
        copy.start()
    barrier = pltpu.get_barrier_semaphore()
    for ds, dy, dx in partners:
        def greet(ds=ds, dy=dy, dx=dx):
            pl.semaphore_signal(barrier, inc=1, device_id=target(ds, dy, dx), device_id_type=MESH)
        when_to(dy, greet)

    lane = lax.broadcasted_iota(jnp.int32, (8, 128), 1)
    sub = lax.broadcasted_iota(jnp.int32, (8, 128), 0)

    first = sec == 0
    for copy in loads[:3]:
        copy.wait()
    sea = maskv[...].astype(f32)
    for q in range(2):
        for p in range(levels):
            own[q * levels + p] = curv[q, jnp.where(first, p, levels - 1 - p)] * sea
    edges[0] = sea
    edges[1] = diffv[...]
    n_fld, n_sum = 2 * levels, 10

    loads[3].wait()

    def pack_freq(f, chunk, fi):
        base = f * (dirs * 8)
        for side, start_dir, row in ((0, north_dirs[0], 7), (1, south_dirs[0], 0)):
            for start, count in ((0, 8), (8, 8), (half - 8, 8)):
                at = base + (start_dir + start) * 8 + row
                send_rows[side, chunk, fi * half + start:fi * half + start + count, :] = spec[
                    pl.ds(at, count, stride=8), :
                ]

    for f in range(freqs):
        pack_freq(f, f // per_chunk, f % per_chunk)

    def pack_group(g, _):
        def one(m, accs):
            f = jnp.minimum(g * per_group + m, freqs - 1)
            base = f * (dirs * 8)
            out = []
            for side, chosen, extra in ((0, east_dirs, 1), (1, west_dirs, 0)):
                acc = jnp.zeros((8, 128), f32)
                for j, d in enumerate(chosen):
                    tile = spec[pl.ds(pl.multiple_of(base + d * 8, 8), 8), :]
                    acc = jnp.where(lane == j, roll(tile, j + extra, 1), acc)
                acc = pltpu.roll(acc, half * m, 1)
                here = (lane >= half * m) & (lane < half * m + half)
                out.append(jnp.where(here, acc, accs[side]))
            return tuple(out)

        zero = jnp.zeros((8, 128), f32)
        a, b = lax.fori_loop(0, per_group, one, (zero, zero))
        send_cols[0, g] = a
        send_cols[1, g] = b
        return 0

    lax.fori_loop(0, groups, pack_group, 0)

    for copy in loads[4:]:
        copy.wait()
    for d in range(dirs):
        table[0, d] = abs(cosines[d])
        table[1, d] = abs(sines[d])
    group = 3

    def weigh(step, _):
        total = [[jnp.zeros((8, 128), f32)] * 4 for _ in range(group)]
        for f in range(freqs):
            a, b, c = stokes[f], stress[f], courant[f]
            ws = [jnp.full((8, 128), w, f32) for w in (a, b, a * c, b * c)]
            for n in range(group):
                at = f * dirs * 8 + (step * group + n) * 8
                tile = spec[pl.ds(pl.multiple_of(at, 8), 8), :]
                total[n] = [t + w * tile for t, w in zip(total[n], ws)]
        for n in range(group):
            for i in range(4):
                acc[i, step * group + n] = total[n][i]
        return 0

    lax.fori_loop(0, dirs // group, weigh, 0)

    gsum = [None] * n_sum
    zero = jnp.zeros((8, 128), f32)
    bases = [
        (c, s, c * c, c * s, s * s) for c, s in zip(cosines, sines)
    ]
    north, south, east, west = [], [], [], []
    for w in range(2):
        mid = [zero] * 5
        ns = [[zero] * 5, [zero] * 5]
        ew = [[zero] * 5, [zero] * 5]
        for d in range(dirs):
            plain, moved = acc[w, d], acc[2 + w, d]
            along_x, along_y = abs(cosines[d]), abs(sines[d])
            kept = plain - (along_x + along_y) * moved
            to_x, to_y = along_x * moved, along_y * moved
            x, y = 0 if cosines[d] > 0 else 1, 0 if sines[d] > 0 else 1
            for m in range(5):
                mid[m] = mid[m] + bases[d][m] * kept
                ns[y][m] = ns[y][m] + bases[d][m] * to_y
                ew[x][m] = ew[x][m] + bases[d][m] * to_x
        for m in range(5):
            gsum[5 * w + m] = (
                mid[m]
                + jnp.where(sub > 0, roll(ns[0][m], 1, 0), 0.0)
                + jnp.where(sub < 7, roll(ns[1][m], -1, 0), 0.0)
                + jnp.where(lane > 0, roll(ew[0][m], 1, 1), 0.0)
                + jnp.where(lane < 127, roll(ew[1][m], -1, 1), 0.0)
            )
            for i, out in enumerate((ns[0][m], ns[1][m], ew[0][m], ew[1][m])):
                sums[i, 5 * w + m] = out

    half_sum = n_sum // 2
    row_tiles = -(-2 * n_sum // 8)
    first_rows = -(-2 * half_sum // 8)
    n_first = 1 + first_rows + half_sum
    n_pos = 1 + row_tiles + n_sum

    def sum_at(g):
        return 1 + first_rows + g if g < half_sum else n_pos - n_sum + g

    def row_at(g, side):
        at = 2 * g + side
        tile = 1 + at // 8 if at // 8 < first_rows else n_first + at // 8 - first_rows
        return tile, slice(at % 8, at % 8 + 1)

    rims_e_w = zero
    for g in range(n_sum):
        for side, row in ((0, 7), (1, 0)):
            tile_at, rows_at = row_at(g, side)
            pos[tile_at, rows_at, :] = sums[side, g, row:row + 1, :]
        rims_e_w = jnp.where(lane == g, roll(sums[2, g], g - 127, 1), rims_e_w)
        rims_e_w = jnp.where(lane == n_sum + g, roll(sums[3, g], n_sum + g, 1), rims_e_w)
        pos[sum_at(g)] = gsum[g]
    pos[0] = rims_e_w

    def pack_rows(tiles, ref):
        for p in range(len(tiles) // 2):
            (a_up, a_down), (b_up, b_down) = tiles[2 * p], tiles[2 * p + 1]
            ref[0, p] = jnp.where(sub >= 4, b_up, roll(a_up, 4, 0))
            ref[1, p] = jnp.where(sub < 4, a_down, roll(b_down, 4, 0))

    def pack_cols(tiles, ref):
        to_east, to_west = zero, zero
        for i, (te, tw) in enumerate(tiles):
            here = (lane >= 4 * i) & (lane < 4 * i + 4)
            to_east = jnp.where(here, roll(te, 4 * i + 4, 1), to_east)
            to_west = jnp.where(here, roll(tw, 4 * i, 1), to_west)
        ref[0] = to_east
        ref[1] = to_west

    same = [(t, t) for t in [own[i] for i in range(n_fld)] + [edges[0], edges[1]]]
    pack_rows(same, rowpk)
    pack_cols(same, colpk)

    edge = jnp.where(north_ok, 0, 3) + jnp.where(south_ok, 0, 3)
    pl.semaphore_wait(barrier, 9 - edge)

    messages = []

    def message(src, dst, ds, dy, dx):
        messages.append((src, dst, ds, dy, dx))
        return len(messages) - 1

    def make(i):
        src, dst, ds, dy, dx = messages[i]
        return pltpu.make_async_remote_copy(
            src_ref=src, dst_ref=dst, send_sem=send_sem.at[i], recv_sem=recv_sem.at[i],
            device_id=target(ds, dy, dx), device_id_type=MESH,
        )

    def make_short():
        return pltpu.make_async_remote_copy(
            src_ref=pos.at[0:n_first], dst_ref=pos_in.at[0:n_first], send_sem=send_sem.at[0],
            recv_sem=recv_sem.at[0], device_id=target(1, 0, 0), device_id_type=MESH,
        )

    def act(i, sign, short, what):
        if i == 0:
            pl.when(short)(lambda: what(make_short()))
            pl.when(jnp.logical_not(short))(lambda: what(make(i)))
        else:
            when_to(sign * messages[i][3], lambda: what(make(i)))

    def start(i):
        act(i, 1, first, lambda copy: copy.start())

    def wait_recv(i):
        act(i, -1, jnp.logical_not(first), lambda copy: copy.wait_recv())

    def wait_send(i):
        act(i, 1, first, lambda copy: copy.wait_send())

    center = [message(pos, pos_in, 1, 0, 0), message(own, oth, 1, 0, 0)]
    cols = [message(send_cols.at[s], recv_cols.at[s], 0, 0, 1 - 2 * s) for s in range(2)]
    rows = [
        [message(send_rows.at[s, c], recv_rows.at[s, c], 0, 1 - 2 * s, 0) for s in range(2)]
        for c in range(CHUNKS)
    ]

    def edge_messages(row_src, row_dst, col_src, col_dst):
        out = []
        for dy in (-1, 1, 0):
            for s in range(2):
                out.append(message(col_src(dy).at[s], col_dst.at[1 + dy, s], 0, dy, 1 - 2 * s))
        for s in range(2):
            out.append(message(row_src.at[s], row_dst.at[s], 0, 1 - 2 * s, 0))
        return out

    field_edges = edge_messages(rowpk, row_in, lambda dy: colpk, col_in)
    for i in center + cols + sum(rows, []) + field_edges:
        start(i)

    @pl.when(jnp.logical_not(first))
    def _():
        pos_in[n_first:n_pos] = jnp.zeros((n_pos - n_first, 8, 128), f32)

    @pl.when(jnp.logical_not(south_ok))
    def _():
        recv_rows[0] = jnp.zeros(recv_rows.shape[1:], f32)
        for rows_in, cols_in in ((row_in, col_in), (rowc_in, colc_in), (rowo_in, colo_in)):
            rows_in[0] = jnp.zeros(rows_in.shape[1:], f32)
            cols_in[2] = jnp.zeros(cols_in.shape[1:], f32)

    @pl.when(jnp.logical_not(north_ok))
    def _():
        recv_rows[1] = jnp.zeros(recv_rows.shape[1:], f32)
        for rows_in, cols_in in ((row_in, col_in), (rowc_in, colc_in), (rowo_in, colo_in)):
            rows_in[1] = jnp.zeros(rows_in.shape[1:], f32)
            cols_in[0] = jnp.zeros(cols_in.shape[1:], f32)

    for i in cols:
        wait_recv(i)

    def wave(chunk, fi, _):
        f = chunk * per_chunk + fi
        base = f * (dirs * 8)
        speed = jnp.full((8, 128), courant[f], f32)
        g = f // per_group
        m = f - g * per_group
        back = lax.rem(128 - half * m, 128)
        from_west = pltpu.roll(recv_cols[0, g], back, 1)
        from_east = pltpu.roll(recv_cols[1, g], back, 1)
        for d in range(dirs):
            at = pl.ds(pl.multiple_of(base + d * 8, 8), 8)
            tile = spec[at, :]
            if cosines[d] > 0:
                j = east_dirs.index(d)
                beside = jnp.where(lane == 0, roll(from_west, -j, 1), roll(tile, 1, 1))
            else:
                j = west_dirs.index(d)
                beside = jnp.where(lane == 127, roll(from_east, 127 - j, 1), roll(tile, -1, 1))
            if sines[d] > 0:
                row = recv_rows[0, chunk, pl.ds(fi * half + north_dirs.index(d), 1), :]
                along = jnp.where(sub == 0, row, roll(tile, 1, 0))
            else:
                row = recv_rows[1, chunk, pl.ds(fi * half + south_dirs.index(d), 1), :]
                along = jnp.where(sub == 7, row, roll(tile, -1, 0))
            change = abs(cosines[d]) * (beside - tile) + abs(sines[d]) * (along - tile)
            out_spec[at, :] = tile + speed * change
        return 0

    for c in range(CHUNKS):
        for i in rows[c]:
            wait_recv(i)
        if c < CHUNKS - 1:
            lax.fori_loop(0, per_chunk, functools.partial(wave, c), 0)

    wait_recv(center[0])
    for i in range(n_pos):
        pos_in[i] = pos_in[i] + pos[i]
    rims = pos_in[0]

    def rim_row(g, side):
        tile_at, rows_at = row_at(g, side)
        return pos_in[tile_at, rows_at, :]

    def rim_col(g, side, at):
        return roll(rims, at - n_sum * side - g, 1)

    packed = []
    by_dy = {dy: [] for dy in (-1, 0, 1)}
    for g in range(n_sum):
        tile = pos_in[sum_at(g)]
        to_e, to_w = rim_col(g, 0, 127), rim_col(g, 1, 0)
        up = jnp.where(sub == 7, rim_row(g, 0), roll(tile, -1, 0))
        down = jnp.where(sub == 0, rim_row(g, 1), roll(tile, 1, 0))
        packed.append((up, down))
        pick = lambda t, e, w: (
            jnp.where(lane == 127, e, roll(t, -1, 1)), jnp.where(lane == 0, w, roll(t, 1, 1))
        )
        by_dy[0].append(pick(tile, to_e, to_w))
        by_dy[1].append(pick(up, *(jnp.where(sub == 7, 0.0, roll(t, -1, 0)) for t in (to_e, to_w))))
        by_dy[-1].append(pick(down, *(jnp.where(sub == 0, 0.0, roll(t, 1, 0)) for t in (to_e, to_w))))
    for g in range(n_sum):
        tile = jnp.where(sub == 7, rim_row(g, 0), jnp.where(sub == 0, rim_row(g, 1), 0.0))
        by_dy[0].append((roll(tile, -1, 1), roll(tile, 1, 1)))
    sum_edges = edge_messages(rowc, rowc_in, lambda dy: colc.at[1 + dy], colc_in)
    for n, dy in enumerate((-1, 1, 0)):
        pack_cols(by_dy[dy], colc.at[1 + dy])
        for i in sum_edges[2 * n:2 * n + 2]:
            start(i)
    pack_rows(packed, rowc)
    for s in range(2):
        rowc[s, len(packed) // 2] = rims
    for i in sum_edges[6:]:
        start(i)
    wait_recv(center[1])
    fields = [(oth[i], oth[i]) for i in range(n_fld)]
    oth_edges = edge_messages(rowo, rowo_in, lambda dy: colo, colo_in)
    pack_cols(fields, colo)
    for i in oth_edges[:6]:
        start(i)
    pack_rows(fields, rowo)
    for i in oth_edges[6:]:
        start(i)

    lax.fori_loop(0, per_chunk, functools.partial(wave, CHUNKS - 1), 0)
    su = jnp.where(first, own[0], oth[0])
    sv = jnp.where(first, own[levels], oth[levels])
    for d in range(dirs):
        dop[d] = sea * (1.0 + CURRENT_GAIN * (su * cosines[d] + sv * sines[d]))

    def scale(f, _):
        for d in range(dirs):
            at = pl.ds(pl.multiple_of(f * (dirs * 8) + d * 8, 8), 8)
            out_spec[at, :] = out_spec[at, :] * dop[d]
        return 0

    lax.fori_loop(0, freqs, scale, 0)

    for i in field_edges:
        wait_recv(i)

    def put(ref, index, quads):
        for n, (r, l) in enumerate(((0, 0), (0, 128), (8, 0), (8, 128))):
            ref[index + (slice(r, r + 8), slice(l, l + 128))] = quads[n]

    def ghosts(rows_in, cols_in, i):
        def lanes(dy):
            return jnp.where(
                lane < 4,
                roll(cols_in[1 + dy, 1], -4 * i, 1),
                jnp.where(lane >= 124, roll(cols_in[1 + dy, 0], 124 - 4 * i, 1), 0.0),
            )

        p = i // 2
        if i % 2 == 0:
            low, high = roll(rows_in[0, p], 4, 0), rows_in[1, p]
        else:
            low, high = rows_in[0, p], roll(rows_in[1, p], 4, 0)
        corner = jnp.where(sub < 4, lanes(-1), lanes(1))
        return lanes(0), jnp.where(sub < 4, high, low), corner

    for q in range(2):
        for p in range(levels):
            i = q * levels + p
            put(ext, (q, p), (own[i],) + ghosts(row_in, col_in, i))
    for n in range(2):
        put(aux, (n,), (edges[n],) + ghosts(row_in, col_in, n_fld + n))

    big_sub = lax.broadcasted_iota(jnp.int32, (16, 256), 0)
    row_index = jnp.where(big_sub < 12, big_sub, big_sub - 16) + lat * 8
    aux[2] = 0.05 + 0.1 * (row_index.astype(f32) + 0.5) / (8 * lats)

    for i in sum_edges:
        wait_recv(i)

    def lanes_of(dy, i):
        from_w = roll(colc_in[1 + dy, 0], 125 - 4 * i, 1)
        from_e = roll(colc_in[1 + dy, 1], -4 * i - 1, 1)
        inner = jnp.where(lane == 0, from_w, jnp.where(lane == 127, from_e, 0.0))
        outer = jnp.where(lane < 3, from_e, jnp.where(lane >= 125, from_w, 0.0))
        return inner, outer

    last = n_sum // 2
    far_rims = jnp.where(sub < 3, rowc_in[1, last], jnp.where(sub >= 5, rowc_in[0, last], 0.0))
    total = []
    for g in range(n_sum):
        i = g
        p = i // 2
        inner, outer = lanes_of(0, i)
        low = roll(rowc_in[0, p], 5 if i % 2 == 0 else 1, 0)
        high = roll(rowc_in[1, p], -1 if i % 2 == 0 else 3, 0)
        s_inner, s_outer = (roll(t, 1, 0) for t in lanes_of(1, i))
        n_inner, n_outer = (roll(t, -1, 0) for t in lanes_of(-1, i))
        low, high = low + s_inner, high + n_inner
        mine_out = jnp.where(
            lane == 0, rim_col(g, 0, 0), jnp.where(lane == 127, rim_col(g, 1, 127), 0.0)
        )
        mine_rows = jnp.where(sub == 0, rim_row(g, 0), jnp.where(sub == 7, rim_row(g, 1), 0.0))
        beside = lanes_of(0, n_sum + g)[1]
        corner = jnp.where(
            sub == 0, roll(beside, 1, 0), jnp.where(sub == 7, roll(beside, -1, 0), 0.0)
        ) + jnp.where(
            lane == 0, roll(far_rims, -g, 1),
            jnp.where(lane == 127, roll(far_rims, 127 - n_sum - g, 1), 0.0),
        )
        edge_rows = lambda a, b: jnp.where(sub == 0, a, jnp.where(sub == 7, b, 0.0))
        out_rows = lambda a, b: jnp.where(sub < 3, b, jnp.where(sub >= 5, a, 0.0))
        total.append((
            pos_in[sum_at(g)] + inner + edge_rows(low, high),
            mine_out + outer + edge_rows(s_outer, n_outer),
            mine_rows + out_rows(low, high),
            corner + out_rows(s_outer, n_outer),
        ))
    for i in oth_edges:
        wait_recv(i)
    for q in range(2):
        for p in range(levels):
            i = q * levels + p
            put(ext, (q, 2 * levels - 1 - p), (oth[i],) + ghosts(rowo_in, colo_in, i))
    surface_at = jnp.where(first, 0, 2 * levels - 1)
    for n, (r, l) in enumerate(((0, 0), (0, 128), (8, 0), (8, 128))):
        at = (slice(r, r + 8), slice(l, l + 128))
        su = CURRENT_GAIN * ext[(0, surface_at) + at]
        sv = CURRENT_GAIN * ext[(1, surface_at) + at]
        for w in range(2):
            c, s, cc, cs, ss = (total[5 * w + m][n] for m in range(5))
            frc[(2 * w,) + at] = aux[(0,) + at] * (c + su * cc + sv * cs)
            frc[(2 * w + 1,) + at] = aux[(0,) + at] * (s + su * cs + sv * ss)
    for i in range(len(messages)):
        wait_send(i)


def level_of(first, total, p):
    return jnp.where(first, p, total - 1 - p)


def forcing(aux, frc, first, total, p):
    k = level_of(first, total, p)
    decay = aux[2] / (1.0 + k.astype(f32))
    top = jnp.where(k == 0, STRESS_GAIN, 0.0)
    return decay * frc[1] + top * frc[2], top * frc[3] - decay * frc[0]


def ocean_level(src, dst, aux, frc, first, total, p):
    k = level_of(first, total, p)
    mix = 0.04 + 0.0125 * lax.rem(7 * k, 5).astype(f32)
    center = [src[0, p], src[1, p]]
    new = []
    for q in range(2):
        mid = center[q]
        lap = (
            roll(mid, -1, 0) + roll(mid, 1, 0) + roll(mid, -1, 1) + roll(mid, 1, 1) - 4.0 * mid
        )
        vert = src[q, p + 1] - mid
        if not (isinstance(p, int) and p == 0):
            vert = vert + (src[q, p - 1] - mid)
        new.append(mid + aux[1] * lap + mix * vert)
    new[0] = new[0] + aux[2] * center[1]
    new[1] = new[1] - aux[2] * center[0]
    if frc is not None:
        force = forcing(aux, frc, first, total, p)
        new = [new[0] + force[0], new[1] + force[1]]
    for q in range(2):
        if dst.shape[-1] == 256:
            dst[q, p] = aux[0] * new[q]
        else:
            own = jnp.where(first, p, dst.shape[1] - 1 - p)
            dst[q, own] = (aux[0] * new[q])[0:8, 0:128]


def emit(levels, spec, ext, aux, frc, out_spec, out_cur, fa, fb, cur, sems):
    part = spec.shape[0] // EMIT
    copies = []
    for i in range(EMIT):
        at = pl.ds(i * part, part)
        copies.append(pltpu.make_async_copy(spec.at[at], out_spec.at[at], sems.at[i]))
    for copy in copies:
        copy.start()
    first = lax.axis_index("sec") == 0
    total = 2 * levels
    src, dst = ext, fa
    for step in range(ITERS):
        for p in range(total - 1 - step):
            ocean_level(src, cur if step == ITERS - 1 else dst, aux, frc, first, total, p)
        src, dst = dst, fb if dst is fa else fa
    last = pltpu.make_async_copy(cur, out_cur, sems.at[EMIT])
    last.start()
    for copy in copies:
        copy.wait()
    last.wait()


def shards(lats, lons, spectra, currents, land_mask, diffusion, courant, stokes_weight, stress_weight):
    freqs, dirs, tile_rows, tile_cols = spectra.shape
    levels = currents.shape[1]
    cells = freqs * dirs * tile_rows
    half = dirs // 2
    rows = -(-freqs // CHUNKS * half // 8) * 8
    groups = -(-freqs // (128 // half))
    tile = (8, 128)
    vmem = lambda *shape: pltpu.VMEM(shape, f32)
    any_spec = pl.BlockSpec(memory_space=pl.ANY)
    n_msg = 4 + 2 * CHUNKS + 24
    big = (2, 2 * levels, 16, 256)
    vmem_spec = pl.BlockSpec(memory_space=pltpu.VMEM)
    results = pl.pallas_call(
        functools.partial(kernel, freqs, dirs, levels, lats, lons),
        out_shape=(vmem(cells, 128), vmem(*big), vmem(3, 16, 256), vmem(4, 16, 256)),
        in_specs=[any_spec] * 7,
        out_specs=(vmem_spec,) * 4,
        scratch_shapes=[
            vmem(cells, 128), vmem(2, levels, *tile),
            pltpu.VMEM(tile, jnp.int32), vmem(*tile),
            pltpu.SMEM((freqs,), f32), pltpu.SMEM((freqs,), f32), pltpu.SMEM((freqs,), f32),
            pltpu.SMEM((2, dirs), f32),
            vmem(2, CHUNKS, rows, 128), vmem(2, CHUNKS, rows, 128),
            vmem(2, groups, *tile), vmem(2, groups, *tile),
            vmem(2 * levels, *tile), vmem(2 * levels, *tile), vmem(2, *tile),
            vmem(2, levels + 1, *tile), vmem(2, levels + 1, *tile),
            vmem(2, *tile), vmem(3, 2, *tile),
            vmem(14, *tile), vmem(14, *tile),
            vmem(2, 6, *tile), vmem(2, 6, *tile), vmem(3, 2, *tile), vmem(3, 2, *tile),
            vmem(2, levels, *tile), vmem(2, levels, *tile), vmem(2, *tile), vmem(3, 2, *tile),
            vmem(dirs, *tile), vmem(4, dirs, *tile), vmem(4, 10, *tile),
            pltpu.SemaphoreType.DMA((7,)),
            pltpu.SemaphoreType.DMA((n_msg,)),
            pltpu.SemaphoreType.DMA((n_msg,)),
        ],
        compiler_params=pltpu.CompilerParams(collective_id=0, has_side_effects=True),
        name="window",
    )(spectra.reshape(cells, tile_cols), currents, land_mask, diffusion, courant, stokes_weight, stress_weight)
    results = [pltpu.with_memory_space_constraint(r, pltpu.VMEM) for r in results]
    new_spectra, new_currents = pl.pallas_call(
        functools.partial(emit, levels),
        out_shape=(
            jax.ShapeDtypeStruct((cells, tile_cols), f32),
            jax.ShapeDtypeStruct(currents.shape, f32),
        ),
        in_specs=[vmem_spec] * 4,
        out_specs=(any_spec, any_spec),
        scratch_shapes=[
            vmem(*big), vmem(*big), vmem(2, levels, *tile), pltpu.SemaphoreType.DMA((EMIT + 1,)),
        ],
        name="emit",
    )(*results)
    return new_spectra.reshape(spectra.shape), new_currents


def solution(mesh):
    in_specs = (
        P("sec", None, "lat", "lon"),
        P(None, "sec", "lat", "lon"),
        P("lat", "lon"),
        P("lat", "lon"),
        P("sec"),
        P("sec"),
        P("sec"),
    )
    out_specs = (P("sec", None, "lat", "lon"), P(None, "sec", "lat", "lon"))
    body = functools.partial(shards, mesh.shape["lat"], mesh.shape["lon"])
    return jax.shard_map(body, mesh=mesh, in_specs=in_specs, out_specs=out_specs, check_vma=False)
```

```python
import functools
import math

import jax
import jax.numpy as jnp
import numpy as np
from jax import lax
from jax.experimental import pallas as pl
from jax.experimental.pallas import tpu as pltpu
from jax.sharding import PartitionSpec as P

ITERS = 4
CURRENT_GAIN = 0.1
STRESS_GAIN = 0.5
MESH = pl.DeviceIdType.MESH
f32 = jnp.float32
CHUNKS = 3
EMIT = 4


def headings(directions):
    heading = ((np.arange(directions).astype(np.float32) + np.float32(0.5))
               * np.float32(2.0 * math.pi / directions)).astype(np.float64)
    return [float(np.float32(c)) for c in np.cos(heading)], [float(np.float32(s)) for s in np.sin(heading)]


def roll(x, shift, axis):
    shift = shift % x.shape[axis]
    return x if shift == 0 else pltpu.roll(x, shift, axis)


def kernel(
    freqs, dirs, levels, lats, lons,
    spec_hbm, cur_hbm, mask_hbm, diff_hbm, courant_hbm, stokes_hbm, stress_hbm,
    out_spec, ext, aux, gtot, oth, rowo_in, colo_in,
    spec, curv, maskv, diffv, courant, stokes, stress, table,
    send_rows, recv_rows, send_cols, recv_cols,
    own, edges, rowpk, row_in, colpk, col_in,
    pos, pos_in, rowc, rowc_in, colc, colc_in, rowo, colo,
    dop, acc, sums,
    local_sem, send_sem, recv_sem,
):
    sec, lat, lon = lax.axis_index("sec"), lax.axis_index("lat"), lax.axis_index("lon")
    north_ok, south_ok = lat < lats - 1, lat > 0
    cosines, sines = headings(dirs)
    east_dirs = [d for d in range(dirs) if cosines[d] > 0]
    west_dirs = [d for d in range(dirs) if cosines[d] <= 0]
    north_dirs = [d for d in range(dirs) if sines[d] > 0]
    south_dirs = [d for d in range(dirs) if sines[d] <= 0]
    half = dirs // 2
    per_chunk = freqs // CHUNKS
    per_group = 128 // half
    groups = -(-freqs // per_group)

    def target(dsec, dlat, dlon):
        return (
            lax.rem(sec + dsec, 2),
            lat + dlat,
            lax.rem(lon + dlon + lons, lons),
        )

    def when_to(dlat, fn):
        if dlat == 0:
            fn()
        else:
            pl.when(north_ok if dlat > 0 else south_ok)(fn)

    partners = [
        (ds, dy, dx) for ds in (0, 1) for dy in (-1, 0, 1) for dx in (-1, 0, 1)
        if (ds, dy, dx) == (1, 0, 0) or (ds == 0 and (dy, dx) != (0, 0))
    ]
    loads = [
        pltpu.make_async_copy(cur_hbm, curv, local_sem.at[0]),
        pltpu.make_async_copy(mask_hbm, maskv, local_sem.at[1]),
        pltpu.make_async_copy(diff_hbm, diffv, local_sem.at[2]),
        pltpu.make_async_copy(spec_hbm, spec, local_sem.at[3]),
        pltpu.make_async_copy(courant_hbm, courant, local_sem.at[4]),
        pltpu.make_async_copy(stokes_hbm, stokes, local_sem.at[5]),
        pltpu.make_async_copy(stress_hbm, stress, local_sem.at[6]),
    ]
    for copy in loads:
        copy.start()
    barrier = pltpu.get_barrier_semaphore()
    for ds, dy, dx in partners:
        def greet(ds=ds, dy=dy, dx=dx):
            pl.semaphore_signal(barrier, inc=1, device_id=target(ds, dy, dx), device_id_type=MESH)
        when_to(dy, greet)

    lane = lax.broadcasted_iota(jnp.int32, (8, 128), 1)
    sub = lax.broadcasted_iota(jnp.int32, (8, 128), 0)

    first = sec == 0
    for copy in loads[:3]:
        copy.wait()
    sea = maskv[...].astype(f32)
    for q in range(2):
        for p in range(levels):
            own[q * levels + p] = curv[q, jnp.where(first, p, levels - 1 - p)] * sea
    edges[0] = sea
    edges[1] = diffv[...]
    n_fld, n_sum = 2 * levels, 10

    loads[3].wait()

    def pack_freq(f, chunk, fi):
        base = f * (dirs * 8)
        for side, start_dir, row in ((0, north_dirs[0], 7), (1, south_dirs[0], 0)):
            for start, count in ((0, 8), (8, 8), (half - 8, 8)):
                at = base + (start_dir + start) * 8 + row
                send_rows[side, chunk, fi * half + start:fi * half + start + count, :] = spec[
                    pl.ds(at, count, stride=8), :
                ]

    for f in range(freqs):
        pack_freq(f, f // per_chunk, f % per_chunk)

    def pack_group(g, _):
        def one(m, accs):
            f = jnp.minimum(g * per_group + m, freqs - 1)
            base = f * (dirs * 8)
            out = []
            for side, chosen, extra in ((0, east_dirs, 1), (1, west_dirs, 0)):
                acc = jnp.zeros((8, 128), f32)
                for j, d in enumerate(chosen):
                    tile = spec[pl.ds(pl.multiple_of(base + d * 8, 8), 8), :]
                    acc = jnp.where(lane == j, roll(tile, j + extra, 1), acc)
                acc = pltpu.roll(acc, half * m, 1)
                here = (lane >= half * m) & (lane < half * m + half)
                out.append(jnp.where(here, acc, accs[side]))
            return tuple(out)

        zero = jnp.zeros((8, 128), f32)
        a, b = lax.fori_loop(0, per_group, one, (zero, zero))
        send_cols[0, g] = a
        send_cols[1, g] = b
        return 0

    lax.fori_loop(0, groups, pack_group, 0)

    for copy in loads[4:]:
        copy.wait()
    for d in range(dirs):
        table[0, d] = abs(cosines[d])
        table[1, d] = abs(sines[d])
    group = 3

    def weigh(step, _):
        total = [[jnp.zeros((8, 128), f32)] * 4 for _ in range(group)]
        for f in range(freqs):
            a, b, c = stokes[f], stress[f], courant[f]
            ws = [jnp.full((8, 128), w, f32) for w in (a, b, a * c, b * c)]
            for n in range(group):
                at = f * dirs * 8 + (step * group + n) * 8
                tile = spec[pl.ds(pl.multiple_of(at, 8), 8), :]
                total[n] = [t + w * tile for t, w in zip(total[n], ws)]
        for n in range(group):
            for i in range(4):
                acc[i, step * group + n] = total[n][i]
        return 0

    lax.fori_loop(0, dirs // group, weigh, 0)

    gsum = [None] * n_sum
    zero = jnp.zeros((8, 128), f32)
    bases = [
        (c, s, c * c, c * s, s * s) for c, s in zip(cosines, sines)
    ]
    north, south, east, west = [], [], [], []
    for w in range(2):
        mid = [zero] * 5
        ns = [[zero] * 5, [zero] * 5]
        ew = [[zero] * 5, [zero] * 5]
        for d in range(dirs):
            plain, moved = acc[w, d], acc[2 + w, d]
            along_x, along_y = abs(cosines[d]), abs(sines[d])
            kept = plain - (along_x + along_y) * moved
            to_x, to_y = along_x * moved, along_y * moved
            x, y = 0 if cosines[d] > 0 else 1, 0 if sines[d] > 0 else 1
            for m in range(5):
                mid[m] = mid[m] + bases[d][m] * kept
                ns[y][m] = ns[y][m] + bases[d][m] * to_y
                ew[x][m] = ew[x][m] + bases[d][m] * to_x
        for m in range(5):
            gsum[5 * w + m] = (
                mid[m]
                + jnp.where(sub > 0, roll(ns[0][m], 1, 0), 0.0)
                + jnp.where(sub < 7, roll(ns[1][m], -1, 0), 0.0)
                + jnp.where(lane > 0, roll(ew[0][m], 1, 1), 0.0)
                + jnp.where(lane < 127, roll(ew[1][m], -1, 1), 0.0)
            )
            for i, out in enumerate((ns[0][m], ns[1][m], ew[0][m], ew[1][m])):
                sums[i, 5 * w + m] = out

    half_sum = n_sum // 2
    row_tiles = -(-2 * n_sum // 8)
    first_rows = -(-2 * half_sum // 8)
    n_first = 1 + first_rows + half_sum
    n_pos = 1 + row_tiles + n_sum

    def sum_at(g):
        return 1 + first_rows + g if g < half_sum else n_pos - n_sum + g

    def row_at(g, side):
        at = 2 * g + side
        tile = 1 + at // 8 if at // 8 < first_rows else n_first + at // 8 - first_rows
        return tile, slice(at % 8, at % 8 + 1)

    rims_e_w = zero
    for g in range(n_sum):
        for side, row in ((0, 7), (1, 0)):
            tile_at, rows_at = row_at(g, side)
            pos[tile_at, rows_at, :] = sums[side, g, row:row + 1, :]
        rims_e_w = jnp.where(lane == g, roll(sums[2, g], g - 127, 1), rims_e_w)
        rims_e_w = jnp.where(lane == n_sum + g, roll(sums[3, g], n_sum + g, 1), rims_e_w)
        pos[sum_at(g)] = gsum[g]
    pos[0] = rims_e_w

    def pack_rows(tiles, ref):
        for p in range(len(tiles) // 2):
            (a_up, a_down), (b_up, b_down) = tiles[2 * p], tiles[2 * p + 1]
            ref[0, p] = jnp.where(sub >= 4, b_up, roll(a_up, 4, 0))
            ref[1, p] = jnp.where(sub < 4, a_down, roll(b_down, 4, 0))

    def pack_cols(tiles, ref):
        to_east, to_west = zero, zero
        for i, (te, tw) in enumerate(tiles):
            here = (lane >= 4 * i) & (lane < 4 * i + 4)
            to_east = jnp.where(here, roll(te, 4 * i + 4, 1), to_east)
            to_west = jnp.where(here, roll(tw, 4 * i, 1), to_west)
        ref[0] = to_east
        ref[1] = to_west

    same = [(t, t) for t in [own[i] for i in range(n_fld)] + [edges[0], edges[1]]]
    pack_rows(same, rowpk)
    pack_cols(same, colpk)

    edge = jnp.where(north_ok, 0, 3) + jnp.where(south_ok, 0, 3)
    pl.semaphore_wait(barrier, 9 - edge)

    messages = []

    def message(src, dst, ds, dy, dx):
        messages.append((src, dst, ds, dy, dx))
        return len(messages) - 1

    def make(i):
        src, dst, ds, dy, dx = messages[i]
        return pltpu.make_async_remote_copy(
            src_ref=src, dst_ref=dst, send_sem=send_sem.at[i], recv_sem=recv_sem.at[i],
            device_id=target(ds, dy, dx), device_id_type=MESH,
        )

    def make_short():
        return pltpu.make_async_remote_copy(
            src_ref=pos.at[0:n_first], dst_ref=pos_in.at[0:n_first], send_sem=send_sem.at[0],
            recv_sem=recv_sem.at[0], device_id=target(1, 0, 0), device_id_type=MESH,
        )

    def act(i, sign, short, what):
        if i == 0:
            pl.when(short)(lambda: what(make_short()))
            pl.when(jnp.logical_not(short))(lambda: what(make(i)))
        else:
            when_to(sign * messages[i][3], lambda: what(make(i)))

    def start(i):
        act(i, 1, first, lambda copy: copy.start())

    def wait_recv(i):
        act(i, -1, jnp.logical_not(first), lambda copy: copy.wait_recv())

    def wait_send(i):
        act(i, 1, first, lambda copy: copy.wait_send())

    center = [message(pos, pos_in, 1, 0, 0), message(own, oth, 1, 0, 0)]
    cols = [message(send_cols.at[s], recv_cols.at[s], 0, 0, 1 - 2 * s) for s in range(2)]
    rows = [
        [message(send_rows.at[s, c], recv_rows.at[s, c], 0, 1 - 2 * s, 0) for s in range(2)]
        for c in range(CHUNKS)
    ]

    def edge_messages(row_src, row_dst, col_src, col_dst):
        out = []
        for dy in (-1, 1, 0):
            for s in range(2):
                out.append(message(col_src(dy).at[s], col_dst.at[1 + dy, s], 0, dy, 1 - 2 * s))
        for s in range(2):
            out.append(message(row_src.at[s], row_dst.at[s], 0, 1 - 2 * s, 0))
        return out

    field_edges = edge_messages(rowpk, row_in, lambda dy: colpk, col_in)
    for i in center + cols + sum(rows, []) + field_edges:
        start(i)

    @pl.when(jnp.logical_not(first))
    def _():
        pos_in[n_first:n_pos] = jnp.zeros((n_pos - n_first, 8, 128), f32)

    @pl.when(jnp.logical_not(south_ok))
    def _():
        recv_rows[0] = jnp.zeros(recv_rows.shape[1:], f32)
        for rows_in, cols_in in ((row_in, col_in), (rowc_in, colc_in), (rowo_in, colo_in)):
            rows_in[0] = jnp.zeros(rows_in.shape[1:], f32)
            cols_in[2] = jnp.zeros(cols_in.shape[1:], f32)

    @pl.when(jnp.logical_not(north_ok))
    def _():
        recv_rows[1] = jnp.zeros(recv_rows.shape[1:], f32)
        for rows_in, cols_in in ((row_in, col_in), (rowc_in, colc_in), (rowo_in, colo_in)):
            rows_in[1] = jnp.zeros(rows_in.shape[1:], f32)
            cols_in[0] = jnp.zeros(cols_in.shape[1:], f32)

    for i in cols:
        wait_recv(i)

    def wave(chunk, fi, _):
        f = chunk * per_chunk + fi
        base = f * (dirs * 8)
        speed = jnp.full((8, 128), courant[f], f32)
        g = f // per_group
        m = f - g * per_group
        back = lax.rem(128 - half * m, 128)
        from_west = pltpu.roll(recv_cols[0, g], back, 1)
        from_east = pltpu.roll(recv_cols[1, g], back, 1)
        for d in range(dirs):
            at = pl.ds(pl.multiple_of(base + d * 8, 8), 8)
            tile = spec[at, :]
            if cosines[d] > 0:
                j = east_dirs.index(d)
                beside = jnp.where(lane == 0, roll(from_west, -j, 1), roll(tile, 1, 1))
            else:
                j = west_dirs.index(d)
                beside = jnp.where(lane == 127, roll(from_east, 127 - j, 1), roll(tile, -1, 1))
            if sines[d] > 0:
                row = recv_rows[0, chunk, pl.ds(fi * half + north_dirs.index(d), 1), :]
                along = jnp.where(sub == 0, row, roll(tile, 1, 0))
            else:
                row = recv_rows[1, chunk, pl.ds(fi * half + south_dirs.index(d), 1), :]
                along = jnp.where(sub == 7, row, roll(tile, -1, 0))
            change = abs(cosines[d]) * (beside - tile) + abs(sines[d]) * (along - tile)
            out_spec[at, :] = tile + speed * change
        return 0

    for c in range(CHUNKS):
        for i in rows[c]:
            wait_recv(i)
        if c < CHUNKS - 1:
            lax.fori_loop(0, per_chunk, functools.partial(wave, c), 0)

    wait_recv(center[0])
    for i in range(n_pos):
        pos_in[i] = pos_in[i] + pos[i]
    rims = pos_in[0]

    def rim_row(g, side):
        tile_at, rows_at = row_at(g, side)
        return pos_in[tile_at, rows_at, :]

    def rim_col(g, side, at):
        return roll(rims, at - n_sum * side - g, 1)

    packed = []
    by_dy = {dy: [] for dy in (-1, 0, 1)}
    for g in range(n_sum):
        tile = pos_in[sum_at(g)]
        to_e, to_w = rim_col(g, 0, 127), rim_col(g, 1, 0)
        up = jnp.where(sub == 7, rim_row(g, 0), roll(tile, -1, 0))
        down = jnp.where(sub == 0, rim_row(g, 1), roll(tile, 1, 0))
        packed.append((up, down))
        pick = lambda t, e, w: (
            jnp.where(lane == 127, e, roll(t, -1, 1)), jnp.where(lane == 0, w, roll(t, 1, 1))
        )
        by_dy[0].append(pick(tile, to_e, to_w))
        by_dy[1].append(pick(up, *(jnp.where(sub == 7, 0.0, roll(t, -1, 0)) for t in (to_e, to_w))))
        by_dy[-1].append(pick(down, *(jnp.where(sub == 0, 0.0, roll(t, 1, 0)) for t in (to_e, to_w))))
    for g in range(n_sum):
        tile = jnp.where(sub == 7, rim_row(g, 0), jnp.where(sub == 0, rim_row(g, 1), 0.0))
        by_dy[0].append((roll(tile, -1, 1), roll(tile, 1, 1)))
    sum_edges = edge_messages(rowc, rowc_in, lambda dy: colc.at[1 + dy], colc_in)
    for n, dy in enumerate((-1, 1, 0)):
        pack_cols(by_dy[dy], colc.at[1 + dy])
        for i in sum_edges[2 * n:2 * n + 2]:
            start(i)
    pack_rows(packed, rowc)
    for s in range(2):
        rowc[s, len(packed) // 2] = rims
    for i in sum_edges[6:]:
        start(i)
    wait_recv(center[1])
    fields = [(oth[i], oth[i]) for i in range(n_fld)]
    oth_edges = edge_messages(rowo, rowo_in, lambda dy: colo, colo_in)
    pack_cols(fields, colo)
    for i in oth_edges[:6]:
        start(i)
    pack_rows(fields, rowo)
    for i in oth_edges[6:]:
        start(i)

    lax.fori_loop(0, per_chunk, functools.partial(wave, CHUNKS - 1), 0)
    su = jnp.where(first, own[0], oth[0])
    sv = jnp.where(first, own[levels], oth[levels])
    for d in range(dirs):
        dop[d] = sea * (1.0 + CURRENT_GAIN * (su * cosines[d] + sv * sines[d]))

    def scale(f, _):
        for d in range(dirs):
            at = pl.ds(pl.multiple_of(f * (dirs * 8) + d * 8, 8), 8)
            out_spec[at, :] = out_spec[at, :] * dop[d]
        return 0

    lax.fori_loop(0, freqs, scale, 0)

    for i in field_edges:
        wait_recv(i)

    for q in range(2):
        for p in range(levels):
            i = q * levels + p
            put(ext, (q, p), (own[i],) + ghosts(row_in, col_in, i))
    for n in range(2):
        put(aux, (n,), (edges[n],) + ghosts(row_in, col_in, n_fld + n))

    big_sub = lax.broadcasted_iota(jnp.int32, (16, 256), 0)
    row_index = jnp.where(big_sub < 12, big_sub, big_sub - 16) + lat * 8
    aux[2] = 0.05 + 0.1 * (row_index.astype(f32) + 0.5) / (8 * lats)

    for i in sum_edges:
        wait_recv(i)

    def lanes_of(dy, i):
        from_w = roll(colc_in[1 + dy, 0], 125 - 4 * i, 1)
        from_e = roll(colc_in[1 + dy, 1], -4 * i - 1, 1)
        inner = jnp.where(lane == 0, from_w, jnp.where(lane == 127, from_e, 0.0))
        outer = jnp.where(lane < 3, from_e, jnp.where(lane >= 125, from_w, 0.0))
        return inner, outer

    last = n_sum // 2
    far_rims = jnp.where(sub < 3, rowc_in[1, last], jnp.where(sub >= 5, rowc_in[0, last], 0.0))
    total = []
    for g in range(n_sum):
        i = g
        p = i // 2
        inner, outer = lanes_of(0, i)
        low = roll(rowc_in[0, p], 5 if i % 2 == 0 else 1, 0)
        high = roll(rowc_in[1, p], -1 if i % 2 == 0 else 3, 0)
        s_inner, s_outer = (roll(t, 1, 0) for t in lanes_of(1, i))
        n_inner, n_outer = (roll(t, -1, 0) for t in lanes_of(-1, i))
        low, high = low + s_inner, high + n_inner
        mine_out = jnp.where(
            lane == 0, rim_col(g, 0, 0), jnp.where(lane == 127, rim_col(g, 1, 127), 0.0)
        )
        mine_rows = jnp.where(sub == 0, rim_row(g, 0), jnp.where(sub == 7, rim_row(g, 1), 0.0))
        beside = lanes_of(0, n_sum + g)[1]
        corner = jnp.where(
            sub == 0, roll(beside, 1, 0), jnp.where(sub == 7, roll(beside, -1, 0), 0.0)
        ) + jnp.where(
            lane == 0, roll(far_rims, -g, 1),
            jnp.where(lane == 127, roll(far_rims, 127 - n_sum - g, 1), 0.0),
        )
        edge_rows = lambda a, b: jnp.where(sub == 0, a, jnp.where(sub == 7, b, 0.0))
        out_rows = lambda a, b: jnp.where(sub < 3, b, jnp.where(sub >= 5, a, 0.0))
        total.append((
            pos_in[sum_at(g)] + inner + edge_rows(low, high),
            mine_out + outer + edge_rows(s_outer, n_outer),
            mine_rows + out_rows(low, high),
            corner + out_rows(s_outer, n_outer),
        ))
    for g in range(n_sum):
        put(gtot, (g,), total[g])
    for i in oth_edges:
        wait_recv(i)
    for i in range(len(messages)):
        wait_send(i)


QUADS = ((0, 0), (0, 128), (8, 0), (8, 128))


def put(ref, index, quads):
    for n, (r, l) in enumerate(QUADS):
        ref[index + (slice(r, r + 8), slice(l, l + 128))] = quads[n]


def ghosts(rows_in, cols_in, i):
    lane = lax.broadcasted_iota(jnp.int32, (8, 128), 1)
    sub = lax.broadcasted_iota(jnp.int32, (8, 128), 0)

    def lanes(dy):
        return jnp.where(
            lane < 4,
            roll(cols_in[1 + dy, 1], -4 * i, 1),
            jnp.where(lane >= 124, roll(cols_in[1 + dy, 0], 124 - 4 * i, 1), 0.0),
        )

    p = i // 2
    if i % 2 == 0:
        low, high = roll(rows_in[0, p], 4, 0), rows_in[1, p]
    else:
        low, high = rows_in[0, p], roll(rows_in[1, p], 4, 0)
    corner = jnp.where(sub < 4, lanes(-1), lanes(1))
    return lanes(0), jnp.where(sub < 4, high, low), corner


def level_of(first, total, p):
    return jnp.where(first, p, total - 1 - p)


def forcing(aux, frc, first, total, p):
    k = level_of(first, total, p)
    decay = aux[2] / (1.0 + k.astype(f32))
    top = jnp.where(k == 0, STRESS_GAIN, 0.0)
    return decay * frc[1] + top * frc[2], top * frc[3] - decay * frc[0]


def ocean_level(src, dst, aux, frc, first, total, p):
    k = level_of(first, total, p)
    mix = 0.04 + 0.0125 * lax.rem(7 * k, 5).astype(f32)
    center = [src[0, p], src[1, p]]
    new = []
    for q in range(2):
        mid = center[q]
        lap = (
            roll(mid, -1, 0) + roll(mid, 1, 0) + roll(mid, -1, 1) + roll(mid, 1, 1) - 4.0 * mid
        )
        vert = src[q, p + 1] - mid
        if not (isinstance(p, int) and p == 0):
            vert = vert + (src[q, p - 1] - mid)
        new.append(mid + aux[1] * lap + mix * vert)
    new[0] = new[0] + aux[2] * center[1]
    new[1] = new[1] - aux[2] * center[0]
    if frc is not None:
        force = forcing(aux, frc, first, total, p)
        new = [new[0] + force[0], new[1] + force[1]]
    for q in range(2):
        if dst.shape[-1] == 256:
            dst[q, p] = aux[0] * new[q]
        else:
            own = jnp.where(first, p, dst.shape[1] - 1 - p)
            dst[q, own] = (aux[0] * new[q])[0:8, 0:128]


def emit(levels, spec, ext, aux, gtot, oth, rowo, colo, out_spec, out_cur, fa, fb, frc, cur, sems):
    part = spec.shape[0] // EMIT
    copies = []
    for i in range(EMIT):
        at = pl.ds(i * part, part)
        copies.append(pltpu.make_async_copy(spec.at[at], out_spec.at[at], sems.at[i]))
    for copy in copies:
        copy.start()
    first = lax.axis_index("sec") == 0
    total = 2 * levels
    for q in range(2):
        for p in range(levels):
            i = q * levels + p
            fb[q, p] = ext[q, p]
            put(fb, (q, total - 1 - p), (oth[i],) + ghosts(rowo, colo, i))
    surface_at = jnp.where(first, 0, total - 1)
    su = CURRENT_GAIN * fb[0, surface_at]
    sv = CURRENT_GAIN * fb[1, surface_at]
    for w in range(2):
        c, s, cc, cs, ss = (gtot[5 * w + m] for m in range(5))
        frc[2 * w] = aux[0] * (c + su * cc + sv * cs)
        frc[2 * w + 1] = aux[0] * (s + su * cs + sv * ss)
    src, dst = fb, fa
    for step in range(ITERS):
        for p in range(total - 1 - step):
            ocean_level(src, cur if step == ITERS - 1 else dst, aux, frc, first, total, p)
        src, dst = dst, fb if dst is fa else fa
    last = pltpu.make_async_copy(cur, out_cur, sems.at[EMIT])
    last.start()
    for copy in copies:
        copy.wait()
    last.wait()


def shards(lats, lons, spectra, currents, land_mask, diffusion, courant, stokes_weight, stress_weight):
    freqs, dirs, tile_rows, tile_cols = spectra.shape
    levels = currents.shape[1]
    cells = freqs * dirs * tile_rows
    half = dirs // 2
    rows = -(-freqs // CHUNKS * half // 8) * 8
    groups = -(-freqs // (128 // half))
    tile = (8, 128)
    vmem = lambda *shape: pltpu.VMEM(shape, f32)
    any_spec = pl.BlockSpec(memory_space=pl.ANY)
    n_msg = 4 + 2 * CHUNKS + 24
    big = (2, 2 * levels, 16, 256)
    vmem_spec = pl.BlockSpec(memory_space=pltpu.VMEM)
    results = pl.pallas_call(
        functools.partial(kernel, freqs, dirs, levels, lats, lons),
        out_shape=(
            vmem(cells, 128), vmem(2, levels, 16, 256), vmem(3, 16, 256), vmem(10, 16, 256),
            vmem(2 * levels, *tile), vmem(2, levels, *tile), vmem(3, 2, *tile),
        ),
        in_specs=[any_spec] * 7,
        out_specs=(vmem_spec,) * 7,
        scratch_shapes=[
            vmem(cells, 128), vmem(2, levels, *tile),
            pltpu.VMEM(tile, jnp.int32), vmem(*tile),
            pltpu.SMEM((freqs,), f32), pltpu.SMEM((freqs,), f32), pltpu.SMEM((freqs,), f32),
            pltpu.SMEM((2, dirs), f32),
            vmem(2, CHUNKS, rows, 128), vmem(2, CHUNKS, rows, 128),
            vmem(2, groups, *tile), vmem(2, groups, *tile),
            vmem(2 * levels, *tile), vmem(2, *tile),
            vmem(2, levels + 1, *tile), vmem(2, levels + 1, *tile),
            vmem(2, *tile), vmem(3, 2, *tile),
            vmem(14, *tile), vmem(14, *tile),
            vmem(2, 6, *tile), vmem(2, 6, *tile), vmem(3, 2, *tile), vmem(3, 2, *tile),
            vmem(2, levels, *tile), vmem(2, *tile),
            vmem(dirs, *tile), vmem(4, dirs, *tile), vmem(4, 10, *tile),
            pltpu.SemaphoreType.DMA((7,)),
            pltpu.SemaphoreType.DMA((n_msg,)),
            pltpu.SemaphoreType.DMA((n_msg,)),
        ],
        compiler_params=pltpu.CompilerParams(collective_id=0, has_side_effects=True),
        name="window",
    )(spectra.reshape(cells, tile_cols), currents, land_mask, diffusion, courant, stokes_weight, stress_weight)
    results = [pltpu.with_memory_space_constraint(r, pltpu.VMEM) for r in results]
    new_spectra, new_currents = pl.pallas_call(
        functools.partial(emit, levels),
        out_shape=(
            jax.ShapeDtypeStruct((cells, tile_cols), f32),
            jax.ShapeDtypeStruct(currents.shape, f32),
        ),
        in_specs=[vmem_spec] * 7,
        out_specs=(any_spec, any_spec),
        scratch_shapes=[
            vmem(*big), vmem(*big), vmem(4, 16, 256), vmem(2, levels, *tile), pltpu.SemaphoreType.DMA((EMIT + 1,)),
        ],
        name="emit",
    )(*results)
    return new_spectra.reshape(spectra.shape), new_currents


def solution(mesh):
    in_specs = (
        P("sec", None, "lat", "lon"),
        P(None, "sec", "lat", "lon"),
        P("lat", "lon"),
        P("lat", "lon"),
        P("sec"),
        P("sec"),
        P("sec"),
    )
    out_specs = (P("sec", None, "lat", "lon"), P(None, "sec", "lat", "lon"))
    body = functools.partial(shards, mesh.shape["lat"], mesh.shape["lon"])
    return jax.shard_map(body, mesh=mesh, in_specs=in_specs, out_specs=out_specs, check_vma=False)
```

```python
import functools
import math

import jax
import jax.numpy as jnp
import numpy as np
from jax import lax
from jax.experimental import pallas as pl
from jax.experimental.pallas import tpu as pltpu
from jax.sharding import PartitionSpec as P

ITERS = 4
CURRENT_GAIN = 0.1
STRESS_GAIN = 0.5
MESH = pl.DeviceIdType.MESH
f32 = jnp.float32
CHUNKS = 3
EMIT = 4


def headings(directions):
    heading = ((np.arange(directions).astype(np.float32) + np.float32(0.5))
               * np.float32(2.0 * math.pi / directions)).astype(np.float64)
    return [float(np.float32(c)) for c in np.cos(heading)], [float(np.float32(s)) for s in np.sin(heading)]


def roll(x, shift, axis):
    shift = shift % x.shape[axis]
    return x if shift == 0 else pltpu.roll(x, shift, axis)


def kernel(
    freqs, dirs, levels, lats, lons,
    spec_hbm, cur_hbm, mask_hbm, diff_hbm, courant_hbm, stokes_hbm, stress_hbm,
    out_spec, ext, aux, frc,
    spec, curv, maskv, diffv, courant, stokes, stress, table,
    send_rows, recv_rows, send_cols, recv_cols,
    own, oth, edges, rowpk, row_in, colpk, col_in,
    pos, pos_in, rowc, rowc_in, colc, colc_in, rowo, rowo_in, colo, colo_in,
    dop, acc, sums,
    local_sem, send_sem, recv_sem,
):
    sec, lat, lon = lax.axis_index("sec"), lax.axis_index("lat"), lax.axis_index("lon")
    north_ok, south_ok = lat < lats - 1, lat > 0
    cosines, sines = headings(dirs)
    east_dirs = [d for d in range(dirs) if cosines[d] > 0]
    west_dirs = [d for d in range(dirs) if cosines[d] <= 0]
    north_dirs = [d for d in range(dirs) if sines[d] > 0]
    south_dirs = [d for d in range(dirs) if sines[d] <= 0]
    half = dirs // 2
    per_chunk = freqs // CHUNKS
    per_group = 128 // half
    groups = -(-freqs // per_group)

    def target(dsec, dlat, dlon):
        return (
            lax.rem(sec + dsec, 2),
            lat + dlat,
            lax.rem(lon + dlon + lons, lons),
        )

    def when_to(dlat, fn):
        if dlat == 0:
            fn()
        else:
            pl.when(north_ok if dlat > 0 else south_ok)(fn)

    partners = [
        (ds, dy, dx) for ds in (0, 1) for dy in (-1, 0, 1) for dx in (-1, 0, 1)
        if (ds, dy, dx) == (1, 0, 0) or (ds == 0 and (dy, dx) != (0, 0))
    ]
    loads = [
        pltpu.make_async_copy(cur_hbm, curv, local_sem.at[0]),
        pltpu.make_async_copy(mask_hbm, maskv, local_sem.at[1]),
        pltpu.make_async_copy(diff_hbm, diffv, local_sem.at[2]),
        pltpu.make_async_copy(spec_hbm, spec, local_sem.at[3]),
        pltpu.make_async_copy(courant_hbm, courant, local_sem.at[4]),
        pltpu.make_async_copy(stokes_hbm, stokes, local_sem.at[5]),
        pltpu.make_async_copy(stress_hbm, stress, local_sem.at[6]),
    ]
    for copy in loads:
        copy.start()
    barrier = pltpu.get_barrier_semaphore()
    for ds, dy, dx in partners:
        def greet(ds=ds, dy=dy, dx=dx):
            pl.semaphore_signal(barrier, inc=1, device_id=target(ds, dy, dx), device_id_type=MESH)
        when_to(dy, greet)

    lane = lax.broadcasted_iota(jnp.int32, (8, 128), 1)
    sub = lax.broadcasted_iota(jnp.int32, (8, 128), 0)

    first = sec == 0
    for copy in loads[:3]:
        copy.wait()
    sea = maskv[...].astype(f32)
    for q in range(2):
        for p in range(levels):
            own[q * levels + p] = curv[q, jnp.where(first, p, levels - 1 - p)] * sea
    edges[0] = sea
    edges[1] = diffv[...]
    n_fld, n_sum = 2 * levels, 10

    loads[3].wait()

    def pack_freq(f, chunk, fi):
        base = f * (dirs * 8)
        for side, start_dir, row in ((0, north_dirs[0], 7), (1, south_dirs[0], 0)):
            for start, count in ((0, 8), (8, 8), (half - 8, 8)):
                at = base + (start_dir + start) * 8 + row
                send_rows[side, chunk, fi * half + start:fi * half + start + count, :] = spec[
                    pl.ds(at, count, stride=8), :
                ]

    for f in range(freqs):
        pack_freq(f, f // per_chunk, f % per_chunk)

    def pack_group(g, _):
        def one(m, accs):
            f = jnp.minimum(g * per_group + m, freqs - 1)
            base = f * (dirs * 8)
            out = []
            for side, chosen, extra in ((0, east_dirs, 1), (1, west_dirs, 0)):
                acc = jnp.zeros((8, 128), f32)
                for j, d in enumerate(chosen):
                    tile = spec[pl.ds(pl.multiple_of(base + d * 8, 8), 8), :]
                    acc = jnp.where(lane == j, roll(tile, j + extra, 1), acc)
                acc = pltpu.roll(acc, half * m, 1)
                here = (lane >= half * m) & (lane < half * m + half)
                out.append(jnp.where(here, acc, accs[side]))
            return tuple(out)

        zero = jnp.zeros((8, 128), f32)
        a, b = lax.fori_loop(0, per_group, one, (zero, zero))
        send_cols[0, g] = a
        send_cols[1, g] = b
        return 0

    lax.fori_loop(0, groups, pack_group, 0)

    for copy in loads[4:]:
        copy.wait()
    for d in range(dirs):
        table[0, d] = abs(cosines[d])
        table[1, d] = abs(sines[d])
    group = 3

    def weigh(step, _):
        total = [[jnp.zeros((8, 128), f32)] * 4 for _ in range(group)]
        for f in range(freqs):
            a, b, c = stokes[f], stress[f], courant[f]
            ws = [jnp.full((8, 128), w, f32) for w in (a, b, a * c, b * c)]
            for n in range(group):
                at = f * dirs * 8 + (step * group + n) * 8
                tile = spec[pl.ds(pl.multiple_of(at, 8), 8), :]
                total[n] = [t + w * tile for t, w in zip(total[n], ws)]
        for n in range(group):
            for i in range(4):
                acc[i, step * group + n] = total[n][i]
        return 0

    lax.fori_loop(0, dirs // group, weigh, 0)

    gsum = [None] * n_sum
    zero = jnp.zeros((8, 128), f32)
    bases = [
        (c, s, c * c, c * s, s * s) for c, s in zip(cosines, sines)
    ]
    north, south, east, west = [], [], [], []
    for w in range(2):
        mid = [zero] * 5
        ns = [[zero] * 5, [zero] * 5]
        ew = [[zero] * 5, [zero] * 5]
        for d in range(dirs):
            plain, moved = acc[w, d], acc[2 + w, d]
            along_x, along_y = abs(cosines[d]), abs(sines[d])
            kept = plain - (along_x + along_y) * moved
            to_x, to_y = along_x * moved, along_y * moved
            x, y = 0 if cosines[d] > 0 else 1, 0 if sines[d] > 0 else 1
            for m in range(5):
                mid[m] = mid[m] + bases[d][m] * kept
                ns[y][m] = ns[y][m] + bases[d][m] * to_y
                ew[x][m] = ew[x][m] + bases[d][m] * to_x
        for m in range(5):
            gsum[5 * w + m] = (
                mid[m]
                + jnp.where(sub > 0, roll(ns[0][m], 1, 0), 0.0)
                + jnp.where(sub < 7, roll(ns[1][m], -1, 0), 0.0)
                + jnp.where(lane > 0, roll(ew[0][m], 1, 1), 0.0)
                + jnp.where(lane < 127, roll(ew[1][m], -1, 1), 0.0)
            )
            for i, out in enumerate((ns[0][m], ns[1][m], ew[0][m], ew[1][m])):
                sums[i, 5 * w + m] = out

    half_sum = n_sum // 2
    row_tiles = -(-2 * n_sum // 8)
    first_rows = -(-2 * half_sum // 8)
    n_first = 1 + first_rows + half_sum
    n_pos = 1 + row_tiles + n_sum

    def sum_at(g):
        return 1 + first_rows + g if g < half_sum else n_pos - n_sum + g

    def row_at(g, side):
        at = 2 * g + side
        tile = 1 + at // 8 if at // 8 < first_rows else n_first + at // 8 - first_rows
        return tile, slice(at % 8, at % 8 + 1)

    rims_e_w = zero
    for g in range(n_sum):
        for side, row in ((0, 7), (1, 0)):
            tile_at, rows_at = row_at(g, side)
            pos[tile_at, rows_at, :] = sums[side, g, row:row + 1, :]
        rims_e_w = jnp.where(lane == g, roll(sums[2, g], g - 127, 1), rims_e_w)
        rims_e_w = jnp.where(lane == n_sum + g, roll(sums[3, g], n_sum + g, 1), rims_e_w)
        pos[sum_at(g)] = gsum[g]
    pos[0] = rims_e_w

    def pack_rows(tiles, ref):
        for p in range(len(tiles) // 2):
            (a_up, a_down), (b_up, b_down) = tiles[2 * p], tiles[2 * p + 1]
            ref[0, p] = jnp.where(sub >= 4, b_up, roll(a_up, 4, 0))
            ref[1, p] = jnp.where(sub < 4, a_down, roll(b_down, 4, 0))

    def pack_cols(tiles, ref):
        to_east, to_west = zero, zero
        for i, (te, tw) in enumerate(tiles):
            here = (lane >= 4 * i) & (lane < 4 * i + 4)
            to_east = jnp.where(here, roll(te, 4 * i + 4, 1), to_east)
            to_west = jnp.where(here, roll(tw, 4 * i, 1), to_west)
        ref[0] = to_east
        ref[1] = to_west

    same = [(t, t) for t in [own[i] for i in range(n_fld)] + [edges[0], edges[1]]]
    pack_rows(same, rowpk)
    pack_cols(same, colpk)

    edge = jnp.where(north_ok, 0, 3) + jnp.where(south_ok, 0, 3)
    pl.semaphore_wait(barrier, 9 - edge)

    messages = []

    def message(src, dst, ds, dy, dx):
        messages.append((src, dst, ds, dy, dx))
        return len(messages) - 1

    def make(i):
        src, dst, ds, dy, dx = messages[i]
        return pltpu.make_async_remote_copy(
            src_ref=src, dst_ref=dst, send_sem=send_sem.at[i], recv_sem=recv_sem.at[i],
            device_id=target(ds, dy, dx), device_id_type=MESH,
        )

    def make_short():
        return pltpu.make_async_remote_copy(
            src_ref=pos.at[0:n_first], dst_ref=pos_in.at[0:n_first], send_sem=send_sem.at[0],
            recv_sem=recv_sem.at[0], device_id=target(1, 0, 0), device_id_type=MESH,
        )

    def act(i, sign, short, what):
        if i == 0:
            pl.when(short)(lambda: what(make_short()))
            pl.when(jnp.logical_not(short))(lambda: what(make(i)))
        else:
            when_to(sign * messages[i][3], lambda: what(make(i)))

    def start(i):
        act(i, 1, first, lambda copy: copy.start())

    def wait_recv(i):
        act(i, -1, jnp.logical_not(first), lambda copy: copy.wait_recv())

    def wait_send(i):
        act(i, 1, first, lambda copy: copy.wait_send())

    center = [message(pos, pos_in, 1, 0, 0), message(own, oth, 1, 0, 0)]
    cols = [message(send_cols.at[s], recv_cols.at[s], 0, 0, 1 - 2 * s) for s in range(2)]
    rows = [
        [message(send_rows.at[s, c], recv_rows.at[s, c], 0, 1 - 2 * s, 0) for s in range(2)]
        for c in range(CHUNKS)
    ]

    def edge_messages(row_src, row_dst, col_src, col_dst):
        out = []
        for dy in (-1, 1, 0):
            for s in range(2):
                out.append(message(col_src(dy).at[s], col_dst.at[1 + dy, s], 0, dy, 1 - 2 * s))
        for s in range(2):
            out.append(message(row_src.at[s], row_dst.at[s], 0, 1 - 2 * s, 0))
        return out

    field_edges = edge_messages(rowpk, row_in, lambda dy: colpk, col_in)
    for i in center + cols + sum(rows, []) + field_edges:
        start(i)

    @pl.when(jnp.logical_not(first))
    def _():
        pos_in[n_first:n_pos] = jnp.zeros((n_pos - n_first, 8, 128), f32)

    @pl.when(jnp.logical_not(south_ok))
    def _():
        recv_rows[0] = jnp.zeros(recv_rows.shape[1:], f32)
        for rows_in, cols_in in ((row_in, col_in), (rowc_in, colc_in), (rowo_in, colo_in)):
            rows_in[0] = jnp.zeros(rows_in.shape[1:], f32)
            cols_in[2] = jnp.zeros(cols_in.shape[1:], f32)

    @pl.when(jnp.logical_not(north_ok))
    def _():
        recv_rows[1] = jnp.zeros(recv_rows.shape[1:], f32)
        for rows_in, cols_in in ((row_in, col_in), (rowc_in, colc_in), (rowo_in, colo_in)):
            rows_in[1] = jnp.zeros(rows_in.shape[1:], f32)
            cols_in[0] = jnp.zeros(cols_in.shape[1:], f32)

    for i in cols:
        wait_recv(i)

    def wave(chunk, fi, _):
        f = chunk * per_chunk + fi
        base = f * (dirs * 8)
        speed = jnp.full((8, 128), courant[f], f32)
        g = f // per_group
        m = f - g * per_group
        back = lax.rem(128 - half * m, 128)
        from_west = pltpu.roll(recv_cols[0, g], back, 1)
        from_east = pltpu.roll(recv_cols[1, g], back, 1)
        for d in range(dirs):
            at = pl.ds(pl.multiple_of(base + d * 8, 8), 8)
            tile = spec[at, :]
            if cosines[d] > 0:
                j = east_dirs.index(d)
                beside = jnp.where(lane == 0, roll(from_west, -j, 1), roll(tile, 1, 1))
            else:
                j = west_dirs.index(d)
                beside = jnp.where(lane == 127, roll(from_east, 127 - j, 1), roll(tile, -1, 1))
            if sines[d] > 0:
                row = recv_rows[0, chunk, pl.ds(fi * half + north_dirs.index(d), 1), :]
                along = jnp.where(sub == 0, row, roll(tile, 1, 0))
            else:
                row = recv_rows[1, chunk, pl.ds(fi * half + south_dirs.index(d), 1), :]
                along = jnp.where(sub == 7, row, roll(tile, -1, 0))
            change = abs(cosines[d]) * (beside - tile) + abs(sines[d]) * (along - tile)
            out_spec[at, :] = tile + speed * change
        return 0

    for c in range(CHUNKS):
        for i in rows[c]:
            wait_recv(i)
        if c < CHUNKS - 1:
            lax.fori_loop(0, per_chunk, functools.partial(wave, c), 0)

    wait_recv(center[0])
    for i in range(n_pos):
        pos_in[i] = pos_in[i] + pos[i]
    rims = pos_in[0]

    def rim_row(g, side):
        tile_at, rows_at = row_at(g, side)
        return pos_in[tile_at, rows_at, :]

    def rim_col(g, side, at):
        return roll(rims, at - n_sum * side - g, 1)

    packed = []
    by_dy = {dy: [] for dy in (-1, 0, 1)}
    for g in range(n_sum):
        tile = pos_in[sum_at(g)]
        to_e, to_w = rim_col(g, 0, 127), rim_col(g, 1, 0)
        up = jnp.where(sub == 7, rim_row(g, 0), roll(tile, -1, 0))
        down = jnp.where(sub == 0, rim_row(g, 1), roll(tile, 1, 0))
        packed.append((up, down))
        pick = lambda t, e, w: (
            jnp.where(lane == 127, e, roll(t, -1, 1)), jnp.where(lane == 0, w, roll(t, 1, 1))
        )
        by_dy[0].append(pick(tile, to_e, to_w))
        by_dy[1].append(pick(up, *(jnp.where(sub == 7, 0.0, roll(t, -1, 0)) for t in (to_e, to_w))))
        by_dy[-1].append(pick(down, *(jnp.where(sub == 0, 0.0, roll(t, 1, 0)) for t in (to_e, to_w))))
    for g in range(n_sum):
        tile = jnp.where(sub == 7, rim_row(g, 0), jnp.where(sub == 0, rim_row(g, 1), 0.0))
        by_dy[0].append((roll(tile, -1, 1), roll(tile, 1, 1)))
    sum_edges = edge_messages(rowc, rowc_in, lambda dy: colc.at[1 + dy], colc_in)
    for n, dy in enumerate((-1, 1, 0)):
        pack_cols(by_dy[dy], colc.at[1 + dy])
        for i in sum_edges[2 * n:2 * n + 2]:
            start(i)
    pack_rows(packed, rowc)
    for s in range(2):
        rowc[s, len(packed) // 2] = rims
    for i in sum_edges[6:]:
        start(i)
    wait_recv(center[1])
    fields = [(oth[i], oth[i]) for i in range(n_fld)]
    oth_edges = edge_messages(rowo, rowo_in, lambda dy: colo, colo_in)
    pack_cols(fields, colo)
    for i in oth_edges[:6]:
        start(i)
    pack_rows(fields, rowo)
    for i in oth_edges[6:]:
        start(i)

    lax.fori_loop(0, per_chunk, functools.partial(wave, CHUNKS - 1), 0)
    su = jnp.where(first, own[0], oth[0])
    sv = jnp.where(first, own[levels], oth[levels])
    for d in range(dirs):
        dop[d] = sea * (1.0 + CURRENT_GAIN * (su * cosines[d] + sv * sines[d]))

    def scale(f, _):
        for d in range(dirs):
            at = pl.ds(pl.multiple_of(f * (dirs * 8) + d * 8, 8), 8)
            out_spec[at, :] = out_spec[at, :] * dop[d]
        return 0

    lax.fori_loop(0, freqs, scale, 0)

    for i in field_edges:
        wait_recv(i)

    def put(ref, index, quads):
        for n, (r, l) in enumerate(((0, 0), (0, 128), (8, 0), (8, 128))):
            ref[index + (slice(r, r + 8), slice(l, l + 128))] = quads[n]

    def ghosts(rows_in, cols_in, i):
        def lanes(dy):
            return jnp.where(
                lane < 4,
                roll(cols_in[1 + dy, 1], -4 * i, 1),
                jnp.where(lane >= 124, roll(cols_in[1 + dy, 0], 124 - 4 * i, 1), 0.0),
            )

        p = i // 2
        if i % 2 == 0:
            low, high = roll(rows_in[0, p], 4, 0), rows_in[1, p]
        else:
            low, high = rows_in[0, p], roll(rows_in[1, p], 4, 0)
        corner = jnp.where(sub < 4, lanes(-1), lanes(1))
        return lanes(0), jnp.where(sub < 4, high, low), corner

    for q in range(2):
        for p in range(levels):
            i = q * levels + p
            put(ext, (q, p), (own[i],) + ghosts(row_in, col_in, i))
    for n in range(2):
        put(aux, (n,), (edges[n],) + ghosts(row_in, col_in, n_fld + n))

    big_sub = lax.broadcasted_iota(jnp.int32, (16, 256), 0)
    row_index = jnp.where(big_sub < 12, big_sub, big_sub - 16) + lat * 8
    aux[2] = 0.05 + 0.1 * (row_index.astype(f32) + 0.5) / (8 * lats)

    for i in sum_edges:
        wait_recv(i)

    def lanes_of(dy, i):
        from_w = roll(colc_in[1 + dy, 0], 125 - 4 * i, 1)
        from_e = roll(colc_in[1 + dy, 1], -4 * i - 1, 1)
        inner = jnp.where(lane == 0, from_w, jnp.where(lane == 127, from_e, 0.0))
        outer = jnp.where(lane < 3, from_e, jnp.where(lane >= 125, from_w, 0.0))
        return inner, outer

    last = n_sum // 2
    far_rims = jnp.where(sub < 3, rowc_in[1, last], jnp.where(sub >= 5, rowc_in[0, last], 0.0))
    total = []
    for g in range(n_sum):
        i = g
        p = i // 2
        inner, outer = lanes_of(0, i)
        low = roll(rowc_in[0, p], 5 if i % 2 == 0 else 1, 0)
        high = roll(rowc_in[1, p], -1 if i % 2 == 0 else 3, 0)
        s_inner, s_outer = (roll(t, 1, 0) for t in lanes_of(1, i))
        n_inner, n_outer = (roll(t, -1, 0) for t in lanes_of(-1, i))
        low, high = low + s_inner, high + n_inner
        mine_out = jnp.where(
            lane == 0, rim_col(g, 0, 0), jnp.where(lane == 127, rim_col(g, 1, 127), 0.0)
        )
        mine_rows = jnp.where(sub == 0, rim_row(g, 0), jnp.where(sub == 7, rim_row(g, 1), 0.0))
        beside = lanes_of(0, n_sum + g)[1]
        corner = jnp.where(
            sub == 0, roll(beside, 1, 0), jnp.where(sub == 7, roll(beside, -1, 0), 0.0)
        ) + jnp.where(
            lane == 0, roll(far_rims, -g, 1),
            jnp.where(lane == 127, roll(far_rims, 127 - n_sum - g, 1), 0.0),
        )
        edge_rows = lambda a, b: jnp.where(sub == 0, a, jnp.where(sub == 7, b, 0.0))
        out_rows = lambda a, b: jnp.where(sub < 3, b, jnp.where(sub >= 5, a, 0.0))
        total.append((
            pos_in[sum_at(g)] + inner + edge_rows(low, high),
            mine_out + outer + edge_rows(s_outer, n_outer),
            mine_rows + out_rows(low, high),
            corner + out_rows(s_outer, n_outer),
        ))
    for i in oth_edges:
        wait_recv(i)
    for q in range(2):
        for p in range(levels):
            i = q * levels + p
            put(ext, (q, 2 * levels - 1 - p), (oth[i],) + ghosts(rowo_in, colo_in, i))
    surface_at = jnp.where(first, 0, 2 * levels - 1)
    for n, (r, l) in enumerate(((0, 0), (0, 128), (8, 0), (8, 128))):
        at = (slice(r, r + 8), slice(l, l + 128))
        su = CURRENT_GAIN * ext[(0, surface_at) + at]
        sv = CURRENT_GAIN * ext[(1, surface_at) + at]
        for w in range(2):
            c, s, cc, cs, ss = (total[5 * w + m][n] for m in range(5))
            frc[(2 * w,) + at] = aux[(0,) + at] * (c + su * cc + sv * cs)
            frc[(2 * w + 1,) + at] = aux[(0,) + at] * (s + su * cs + sv * ss)
    for i in range(len(messages)):
        wait_send(i)


def level_of(first, total, p):
    return jnp.where(first, p, total - 1 - p)


def forcing(aux, frc, first, total, p):
    k = level_of(first, total, p)
    decay = aux[2] / (1.0 + k.astype(f32))
    top = jnp.where(k == 0, STRESS_GAIN, 0.0)
    return decay * frc[1] + top * frc[2], top * frc[3] - decay * frc[0]


def ocean_level(src, dst, aux, frc, first, total, p):
    k = level_of(first, total, p)
    mix = 0.04 + 0.0125 * lax.rem(7 * k, 5).astype(f32)
    center = [src[0, p], src[1, p]]
    new = []
    for q in range(2):
        mid = center[q]
        lap = (
            roll(mid, -1, 0) + roll(mid, 1, 0) + roll(mid, -1, 1) + roll(mid, 1, 1) - 4.0 * mid
        )
        vert = src[q, p + 1] - mid
        if not (isinstance(p, int) and p == 0):
            vert = vert + (src[q, p - 1] - mid)
        new.append(mid + aux[1] * lap + mix * vert)
    new[0] = new[0] + aux[2] * center[1]
    new[1] = new[1] - aux[2] * center[0]
    if frc is not None:
        force = forcing(aux, frc, first, total, p)
        new = [new[0] + force[0], new[1] + force[1]]
    for q in range(2):
        if dst.shape[-1] == 256:
            dst[q, p] = aux[0] * new[q]
        else:
            own = jnp.where(first, p, dst.shape[1] - 1 - p)
            dst[q, own] = (aux[0] * new[q])[0:8, 0:128]


def emit(levels, spec, ext, aux, frc, out_spec, out_cur, fa, fb, cur, sems):
    part = spec.shape[0] // EMIT
    copies = []
    for i in range(EMIT):
        at = pl.ds(i * part, part)
        copies.append(pltpu.make_async_copy(spec.at[at], out_spec.at[at], sems.at[i]))
    for i, copy in enumerate(copies):
        copy.start(priority=i % 2)
    first = lax.axis_index("sec") == 0
    total = 2 * levels
    src, dst = ext, fa
    for step in range(ITERS):
        for p in range(total - 1 - step):
            ocean_level(src, cur if step == ITERS - 1 else dst, aux, frc, first, total, p)
        src, dst = dst, fb if dst is fa else fa
    last = pltpu.make_async_copy(cur, out_cur, sems.at[EMIT])
    last.start()
    for copy in copies:
        copy.wait()
    last.wait()


def shards(lats, lons, spectra, currents, land_mask, diffusion, courant, stokes_weight, stress_weight):
    freqs, dirs, tile_rows, tile_cols = spectra.shape
    levels = currents.shape[1]
    cells = freqs * dirs * tile_rows
    half = dirs // 2
    rows = -(-freqs // CHUNKS * half // 8) * 8
    groups = -(-freqs // (128 // half))
    tile = (8, 128)
    vmem = lambda *shape: pltpu.VMEM(shape, f32)
    any_spec = pl.BlockSpec(memory_space=pl.ANY)
    n_msg = 4 + 2 * CHUNKS + 24
    big = (2, 2 * levels, 16, 256)
    vmem_spec = pl.BlockSpec(memory_space=pltpu.VMEM)
    results = pl.pallas_call(
        functools.partial(kernel, freqs, dirs, levels, lats, lons),
        out_shape=(vmem(cells, 128), vmem(*big), vmem(3, 16, 256), vmem(4, 16, 256)),
        in_specs=[any_spec] * 7,
        out_specs=(vmem_spec,) * 4,
        scratch_shapes=[
            vmem(cells, 128), vmem(2, levels, *tile),
            pltpu.VMEM(tile, jnp.int32), vmem(*tile),
            pltpu.SMEM((freqs,), f32), pltpu.SMEM((freqs,), f32), pltpu.SMEM((freqs,), f32),
            pltpu.SMEM((2, dirs), f32),
            vmem(2, CHUNKS, rows, 128), vmem(2, CHUNKS, rows, 128),
            vmem(2, groups, *tile), vmem(2, groups, *tile),
            vmem(2 * levels, *tile), vmem(2 * levels, *tile), vmem(2, *tile),
            vmem(2, levels + 1, *tile), vmem(2, levels + 1, *tile),
            vmem(2, *tile), vmem(3, 2, *tile),
            vmem(14, *tile), vmem(14, *tile),
            vmem(2, 6, *tile), vmem(2, 6, *tile), vmem(3, 2, *tile), vmem(3, 2, *tile),
            vmem(2, levels, *tile), vmem(2, levels, *tile), vmem(2, *tile), vmem(3, 2, *tile),
            vmem(dirs, *tile), vmem(4, dirs, *tile), vmem(4, 10, *tile),
            pltpu.SemaphoreType.DMA((7,)),
            pltpu.SemaphoreType.DMA((n_msg,)),
            pltpu.SemaphoreType.DMA((n_msg,)),
        ],
        compiler_params=pltpu.CompilerParams(collective_id=0, has_side_effects=True),
        name="window",
    )(spectra.reshape(cells, tile_cols), currents, land_mask, diffusion, courant, stokes_weight, stress_weight)
    results = [pltpu.with_memory_space_constraint(r, pltpu.VMEM) for r in results]
    new_spectra, new_currents = pl.pallas_call(
        functools.partial(emit, levels),
        out_shape=(
            jax.ShapeDtypeStruct((cells, tile_cols), f32),
            jax.ShapeDtypeStruct(currents.shape, f32),
        ),
        in_specs=[vmem_spec] * 4,
        out_specs=(any_spec, any_spec),
        scratch_shapes=[
            vmem(*big), vmem(*big), vmem(2, levels, *tile), pltpu.SemaphoreType.DMA((EMIT + 1,)),
        ],
        name="emit",
    )(*results)
    return new_spectra.reshape(spectra.shape), new_currents


def solution(mesh):
    in_specs = (
        P("sec", None, "lat", "lon"),
        P(None, "sec", "lat", "lon"),
        P("lat", "lon"),
        P("lat", "lon"),
        P("sec"),
        P("sec"),
        P("sec"),
    )
    out_specs = (P("sec", None, "lat", "lon"), P(None, "sec", "lat", "lon"))
    body = functools.partial(shards, mesh.shape["lat"], mesh.shape["lon"])
    return jax.shard_map(body, mesh=mesh, in_specs=in_specs, out_specs=out_specs, check_vma=False)
```
